256 devices in a mesh: dom: 8 (over x, core), st: 32 (over y, z).
Axes of the slice: x: 4, y: 4, z: 8, core: 2. Of those that a mesh axis runs over, the one named last changes fastest.
Arguments:
- orbitals: bfloat16 [512, 512, 1024], P('st', 'dom'), may hold values from -6 to 6
- potential: bfloat16 [512, 1024], P('dom'), may hold values from -0.5 to 0.5
- rotation: bfloat16 [512, 512], P('st'), may hold values from -0.25 to 0.25
Outputs:
- rotated: bfloat16 [512, 524288], P(None, ('dom', 'st'))
The draws below stay inside these ranges and needn't reach their ends.
All inputs are finite; a program needn't handle non-finite values.
Results may differ from the reference program's by a relative error of at most 0.0049.
Values may be sent and summed in bfloat16 or wider, within the bound.
No kernel may reach another device: no remote copies, remote signals or barrier semaphores. Data moves between devices by JAX's collectives and lax.ppermute only.
A program may use at most 64 MiB of HBM per device.

```python
import jax
import jax.numpy as jnp
from jax import lax

STATES = 512
DEGREE = 4
NY = 32
NZ = 32
NX = 512


def block_scale(own_key, dims, cuts, low, high):
    gain = 1.0
    for dim, parts in cuts:
        heights = jax.random.uniform(jax.random.fold_in(jax.random.fold_in(own_key, 6), dim), (parts,), jnp.float32, low / len(cuts), high / len(cuts))
        gain = gain * jnp.repeat(jnp.exp(heights), dims[dim] // parts).reshape((-1,) + (1,) * (len(dims) - 1 - dim))
    return gain


def centred(stream_key, extent, scale, most, shards=(), dtype=jnp.bfloat16):
    array = scale * jax.random.normal(stream_key, extent, jnp.float32)
    if shards:
        array = array * block_scale(stream_key, extent, shards, -0.22, 0.18)
    return jnp.clip(array, -most, most).astype(dtype)


def setup_inputs(seed: int = 0) -> dict:
    keys = jax.random.split(jax.random.key(seed), 4)
    orbitals = centred(keys[0], (STATES, NX, NY * NZ), 1.0, 6.0, ((0, 32), (1, 8)))
    potential = jnp.clip(jax.random.uniform(keys[1], (NX, NY * NZ), jnp.float32, -0.5, 0.5) * block_scale(keys[1], (NX, NY * NZ), ((0, 8),), -0.4, 0.0), -0.5, 0.5).astype(jnp.bfloat16)
    rotation = centred(keys[2], (STATES, STATES), STATES ** -0.5, 0.25, ((0, 32),))
    return {"orbitals": orbitals, "potential": potential, "rotation": rotation}


cheb_shift = 3.75
cheb_scale = 3.25


def neighbour_sum(center, nz_count):
    row_width = center.shape[2]
    z_position = lax.broadcasted_iota(jnp.int32, (1, 1, row_width), 2) % nz_count
    padded = jnp.pad(center, ((0, 0), (0, 0), (nz_count, nz_count)))
    along_y = padded[:, :, 2 * nz_count:] + padded[:, :, :row_width]
    upper_z = jnp.where(z_position < nz_count - 1, padded[:, :, nz_count + 1:nz_count + 1 + row_width], 0.0)
    lower_z = jnp.where(z_position > 0, padded[:, :, nz_count - 1:nz_count - 1 + row_width], 0.0)
    return along_y + upper_z + lower_z


def hamiltonian(padded_x, local_pot, nz_count):
    center = padded_x[:, 1:-1]
    beside = padded_x[:, 2:] + padded_x[:, :-2] + neighbour_sum(center, nz_count)
    return (3.0 + local_pot) * center - 0.5 * beside


def chebyshev(start, apply_fn, degree):
    previous = start
    current = (apply_fn(start) - cheb_shift * start) / cheb_scale
    for filter_order in range(1, degree):
        following = 2.0 * (apply_fn(current) - cheb_shift * current) / cheb_scale - previous
        previous = current
        current = following
    return current


def reference(orbitals, potential, rotation):
    local_pot = potential.astype(jnp.float32)

    def apply_fn(state_field):
        return hamiltonian(jnp.pad(state_field, ((0, 0), (1, 1), (0, 0))), local_pot, NZ)

    def filter_block(block):
        return chebyshev(block.astype(jnp.float32), apply_fn, DEGREE).astype(jnp.bfloat16)

    filtered = lax.map(filter_block, orbitals.reshape(STATES // 16, 16, NX, NY * NZ))
    filtered = filtered.reshape(STATES, NX * NY * NZ)

    def rotate_block(rows):
        return jnp.dot(rows, filtered, preferred_element_type=jnp.float32).astype(jnp.bfloat16)

    rotated = lax.map(rotate_block, rotation.reshape(STATES // 16, 16, STATES))
    return rotated.reshape(STATES, NX * NY * NZ)
```

```python
import functools

import jax
import jax.numpy as jnp
from jax import lax
from jax.experimental import pallas as pl
from jax.experimental.pallas import tpu as pltpu
from jax.sharding import PartitionSpec as P

DEGREE = 4
NZ = 32
LANES = 128

cheb_shift = 3.75
cheb_scale = 3.25

F32 = jnp.float32
BF16 = jnp.bfloat16

INNER_Y = LANES // NZ
RUN = NZ + 8
PLANE = INNER_Y * RUN


def one_hot(rows, cols, want):
    r = lax.broadcasted_iota(jnp.int32, (rows, cols), 0)
    c = lax.broadcasted_iota(jnp.int32, (rows, cols), 1)
    return jnp.where(c == want(r), 1.0, 0.0).astype(BF16)


def turned(block):
    eye = one_hot(LANES, LANES, lambda r: r)
    return lax.dot_general(eye, block, (((1,), (1,)), ((), ())), preferred_element_type=F32)


def stacked(rows, states, first, count):
    width = rows.shape[1]
    return jnp.concatenate(
        [
            rows[(first + p) * states : (first + p + 1) * states, j * LANES : (j + 1) * LANES]
            for p in range(count)
            for j in range(width // LANES)
        ],
        axis=0,
    )


def edges_kernel(first_ref, last_ref, pot_first_ref, pot_last_ref, low_ref, high_ref):
    states, slab, width = first_ref.shape
    rows = DEGREE * states
    pick = one_hot(rows, states * slab, lambda r: (r % states) * slab + r // states)
    first = first_ref[...].reshape(states * slab, width)
    low_ref[:rows] = jnp.dot(pick, first, preferred_element_type=F32).astype(BF16)
    low_ref[rows:] = pot_first_ref[...]
    pick = one_hot(
        rows, states * slab, lambda r: (r % states) * slab + r // states + (slab - DEGREE)
    )
    last = last_ref[...].reshape(states * slab, width)
    high_ref[:rows] = jnp.dot(pick, last, preferred_element_type=F32).astype(BF16)
    high_ref[rows:] = pot_last_ref[...]


def edges(orbitals, potential):
    states, planes, width = orbitals.shape
    slab = 8
    last = planes // slab - 1
    out = jax.ShapeDtypeStruct((DEGREE * states + slab, width), BF16)
    return pl.pallas_call(
        edges_kernel,
        grid=(1,),
        in_specs=[
            pl.BlockSpec((states, slab, width), lambda i: (0, 0, 0)),
            pl.BlockSpec((states, slab, width), lambda i: (0, last, 0)),
            pl.BlockSpec((slab, width), lambda i: (0, 0)),
            pl.BlockSpec((slab, width), lambda i: (last, 0)),
        ],
        out_specs=[pl.BlockSpec(out.shape, lambda i: (0, 0))] * 2,
        out_shape=[out, out],
        name="edges",
    )(orbitals, orbitals, potential, potential)


def spread(pot_rows, states):
    count = pot_rows.shape[0]
    repeat = one_hot(count * states, count, lambda r: r // states)
    return jnp.dot(repeat, pot_rows, preferred_element_type=F32).astype(BF16)


def prepare_kernel(x_ref, pot_ref, field_ref, pot_out_ref):
    states, group, width = x_ref.shape
    pick = one_hot(
        states * group, states * group, lambda r: (r % states) * group + r // states
    )
    rows = x_ref[...].reshape(states * group, width)
    rows = jnp.dot(pick, rows, preferred_element_type=F32).astype(BF16)
    pot = spread(pot_ref[...], states)
    for p in range(0, group, 2):
        for source, target in ((rows, field_ref), (pot, pot_out_ref)):
            both = turned(stacked(source, states, p, 2)).astype(BF16)
            target[p] = both[:, :LANES]
            target[p + 1] = both[:, LANES:]


def prepare(orbitals, potential):
    states, planes, width = orbitals.shape
    group = 16
    out = jax.ShapeDtypeStruct((planes, LANES, LANES), BF16)
    return pl.pallas_call(
        prepare_kernel,
        grid=(planes // group,),
        in_specs=[
            pl.BlockSpec((states, group, width), lambda i: (0, i, 0)),
            pl.BlockSpec((group, width), lambda i: (i, 0)),
        ],
        out_specs=[pl.BlockSpec((group, LANES, LANES), lambda i: (i, 0, 0))] * 2,
        out_shape=[out, out],
        cost_estimate=pl.CostEstimate(
            flops=4 * 2 * states * planes * width * 256, transcendentals=0, bytes_accessed=8 << 20
        ),
        name="prepare",
    )(orbitals, potential)


def filter_kernel(
    edge_ref, field_hbm, pot_hbm, low_ref, high_ref, out_hbm,
    even, odd, coef, field_ref, pot_ref, done_ref, out_ref, in_sems, out_sems,
):
    planes = field_ref.shape[0]
    owners, states, points = out_ref.shape
    width = LANES * (LANES // states)
    halo = DEGREE
    b = 1.0 / cheb_scale
    runs = [(r, q) for r in range(INNER_Y) for q in range(NZ // 8)]

    loads = [
        pltpu.make_async_copy(field_hbm, field_ref, in_sems.at[0]),
        pltpu.make_async_copy(pot_hbm, pot_ref, in_sems.at[1]),
    ]
    for load in loads:
        load.start()

    def scaled(p):
        return (p - (cheb_shift - 3.0)) * 2.0

    def put(buffer, plane, values):
        for r in range(INNER_Y):
            at = pl.multiple_of(plane * PLANE + r * RUN + 8, 8)
            buffer[pl.ds(at, NZ), :] = values[r * NZ : (r + 1) * NZ]

    zero = jnp.zeros((8, LANES), F32)

    def clear(i, carry):
        for p in range(4):
            for r in range(INNER_Y):
                at = pl.multiple_of((i * 4 + p) * PLANE + r * RUN, 8)
                even[pl.ds(at, 8), :] = zero
                odd[pl.ds(at, 8), :] = zero
        return carry

    lax.fori_loop(0, (planes + 2 * halo) // 4, clear, 0)
    even[(planes + 2 * halo) * PLANE :, :] = zero
    odd[(planes + 2 * halo) * PLANE :, :] = zero

    rows = DEGREE * states
    for ref, base, at in ((low_ref, 0, 4), (high_ref, halo + planes, 0)):
        field = ref[:rows]
        pot = spread(ref[rows:], states)
        for p in range(0, halo, 2):
            both = turned(stacked(field, states, p, 2))
            put(even, base + p, both[:, :LANES])
            put(even, base + p + 1, both[:, LANES:])
            both = scaled(turned(stacked(pot, states, at + p, 2)))
            coef[base + p] = both[:, :LANES]
            coef[base + p + 1] = both[:, LANES:]

    for load in loads:
        load.wait()

    def fill(i, carry):
        for r in range(2):
            p = i * 2 + r
            put(even, halo + p, field_ref[p].astype(F32))
            coef[halo + p] = scaled(pot_ref[p].astype(F32))
        return carry

    lax.fori_loop(0, planes // 2, fill, 0)

    lane = lax.broadcasted_iota(jnp.int32, (8, LANES), 1)
    first_y = lane < states
    last_y = lane >= LANES - states

    def step(k, plane):
        src, dst = (even, odd) if k % 2 == 1 else (odd, even)
        base = pl.multiple_of(plane * PLANE, 8)

        def rows_at(offset, r, q):
            return src[pl.ds(base + (offset + r * RUN + 8 + q * 8), 8), :]

        here = {rq: rows_at(0, *rq) for rq in runs}
        results = {}
        for r, q in runs:
            v = here[r, q]
            if r > 0:
                below = here[r - 1, q]
            else:
                below = jnp.where(first_y, 0.0, pltpu.roll(here[INNER_Y - 1, q], states, 1))
            if r < INNER_Y - 1:
                above = here[r + 1, q]
            else:
                above = jnp.where(last_y, 0.0, pltpu.roll(here[0, q], LANES - states, 1))
            along_z = rows_at(-1, r, q) + rows_at(1, r, q)
            along_x = rows_at(-PLANE, r, q) + rows_at(PLANE, r, q)
            a = coef[plane, r * NZ + q * 8 : r * NZ + q * 8 + 8, :]
            t = a * v - ((below + above) + (along_z + along_x))
            if k == 1:
                results[r, q] = (0.5 * b) * t
            else:
                results[r, q] = b * t - dst[pl.ds(base + (r * RUN + 8 + q * 8), 8), :]
        return results

    def store(k, plane, results):
        dst = odd if k % 2 == 1 else even
        base = pl.multiple_of(plane * PLANE, 8)
        for r, q in runs:
            dst[pl.ds(base + (r * RUN + 8 + q * 8), 8), :] = results[r, q]

    unroll = 4
    for k in range(1, DEGREE):
        def outer(side, plane, carry, k=k):
            flag = edge_ref[side]
            store(k, plane, {rq: v * flag for rq, v in step(k, plane).items()})
            return carry

        lax.fori_loop(k, halo, functools.partial(outer, 0), 0)
        lax.fori_loop(halo + planes, 2 * halo + planes - k, functools.partial(outer, 1), 0)

        def body(i, carry, k=k):
            results = [step(k, halo + unroll * i + r) for r in range(unroll)]
            for r in range(unroll):
                store(k, halo + unroll * i + r, results[r])
            return carry

        lax.fori_loop(0, planes // unroll, body, 0)

    per = points // width
    batch = unroll // per

    def send(i):
        return pltpu.make_async_copy(
            out_ref.at[pl.ds(i * batch, batch)], out_hbm.at[pl.ds(i * batch, batch)], out_sems.at[i]
        )

    def finish(i):
        for n in range(batch):
            at = pl.multiple_of((i * batch + n) * per * LANES, per * LANES)
            out = turned(done_ref[pl.ds(at, per * LANES), :]).astype(BF16)
            for r in range(per):
                for j in range(width // LANES):
                    out_ref[
                        i * batch + n, :, r * width + j * LANES : r * width + (j + 1) * LANES
                    ] = out[j * states : (j + 1) * states, r * LANES : (r + 1) * LANES]

    def last(i):
        for r in range(unroll):
            res = step(DEGREE, halo + unroll * i + r)
            values = jnp.concatenate([res[rq].astype(BF16) for rq in runs], axis=0)
            at = pl.multiple_of((unroll * i + r) * LANES, LANES)
            done_ref[pl.ds(at, LANES), :] = values

    def both(i, carry):
        finish(i - 1)
        last(i)
        send(i - 1).start()
        return carry

    count = planes // unroll
    last(0)
    lax.fori_loop(1, count, both, 0)
    finish(count - 1)
    send(count - 1).start()
    for i in range(count):
        send(i).wait()


def chebyshev(field, pot, low, high, edge, owners, states):
    planes = field.shape[0]
    points = planes * LANES * LANES // states // owners
    total = planes + 2 * DEGREE
    vmem = pl.BlockSpec(memory_space=pltpu.VMEM)
    anywhere = pl.BlockSpec(memory_space=pl.ANY)
    return pl.pallas_call(
        filter_kernel,
        in_specs=[pl.BlockSpec(memory_space=pltpu.SMEM), anywhere, anywhere, vmem, vmem],
        out_specs=anywhere,
        out_shape=jax.ShapeDtypeStruct((owners, states, points), BF16),
        scratch_shapes=[
            pltpu.VMEM((total * PLANE + 8, LANES), F32),
            pltpu.VMEM((total * PLANE + 8, LANES), F32),
            pltpu.VMEM((total, LANES, LANES), F32),
            pltpu.VMEM(field.shape, BF16),
            pltpu.VMEM(pot.shape, BF16),
            pltpu.VMEM((planes * LANES, LANES), BF16),
            pltpu.VMEM((owners, states, points), BF16),
            pltpu.SemaphoreType.DMA((2,)),
            pltpu.SemaphoreType.DMA((planes // 4,)),
        ],
        name="chebyshev",
    )(edge, field, pot, low, high)


def rotate_kernel(r_ref, f_ref, out_ref):
    out_ref[...] = jnp.dot(r_ref[...], f_ref[...], preferred_element_type=F32).astype(BF16)


def rotate(rotation, filtered):
    total, points = filtered.shape
    tile = 512
    return pl.pallas_call(
        rotate_kernel,
        grid=(points // tile,),
        in_specs=[
            pl.BlockSpec(rotation.shape, lambda i: (0, 0)),
            pl.BlockSpec((total, tile), lambda i: (0, i)),
        ],
        out_specs=pl.BlockSpec((rotation.shape[0], tile), lambda i: (0, i)),
        out_shape=jax.ShapeDtypeStruct((rotation.shape[0], points), BF16),
        name="rotate",
    )(rotation, filtered)


def order_kernel(place_ref, *refs):
    *parts, out_ref = refs
    dom, y, z = place_ref[0], place_ref[1], place_ref[2]
    doms, ys = place_ref[3], place_ref[4]
    total, cols = out_ref.shape
    own = parts[0].shape[0]
    r = lax.broadcasted_iota(jnp.int32, (8, total), 1) // own

    def bit(n):
        return (r >> n) & 1

    source = ((dom + 2 * doms - 4 * bit(2) - 2 * bit(1)) & (doms - 1)) ^ bit(0)
    zs = (z + doms - source) & (doms - 1)
    y_source = (y + 2 * ys - bit(3) - 2 * bit(4)) & (ys - 1)
    want = (y_source * doms + zs) * own
    want = want + lax.broadcasted_iota(jnp.int32, (8, total), 1) % own
    rows = lax.broadcasted_iota(jnp.int32, (total, total), 0)
    pick = jnp.where(rows == jnp.broadcast_to(want[:1], (total, total)), 1.0, 0.0).astype(BF16)
    gathered = jnp.concatenate([p[...] for p in parts], axis=0)
    out_ref[...] = jnp.dot(pick, gathered, preferred_element_type=F32).astype(BF16)


def ordered(place, parts, total):
    vmem = pl.BlockSpec(memory_space=pltpu.VMEM)
    cols = parts[0].shape[1]
    return pl.pallas_call(
        order_kernel,
        in_specs=[pl.BlockSpec(memory_space=pltpu.SMEM)] + [vmem] * len(parts),
        out_specs=vmem,
        out_shape=jax.ShapeDtypeStruct((total, cols), BF16),
        name="order",
    )(place, *parts)


def local(sizes, orbitals, potential, rotation):
    doms, owners = sizes
    zs = doms
    ys = owners // zs
    states = orbitals.shape[0]
    me, spot = lax.axis_index("dom"), lax.axis_index("st")
    up = [(i, i + 1) for i in range(doms - 1)]
    down = [(i + 1, i) for i in range(doms - 1)]
    low_send, high_send = edges(orbitals, potential)
    low = lax.ppermute(high_send, "dom", up)
    high = lax.ppermute(low_send, "dom", down)
    shift = [
        (d * owners + y * zs + z, d * owners + y * zs + (z + d) % zs)
        for d in range(doms)
        for y in range(ys)
        for z in range(zs)
    ]
    rows = lax.ppermute(rotation, ("dom", "st"), shift)
    field, pot = prepare(orbitals, potential)
    rows, field = lax.optimization_barrier((rows, field))
    edge = jnp.stack([me > 0, me < doms - 1]).astype(F32)
    filtered = chebyshev(field, pot, low, high, edge, owners, states)
    rows, _ = lax.optimization_barrier((rows, filtered))
    regrouped = lax.all_to_all(filtered, "st", split_axis=0, concat_axis=0, tiled=True)
    parts = [rows]
    swap = [(i, i ^ 1) for i in range(doms)]
    for perm, axis in (
        (swap, "dom"),
        ([(i, (i + 2) % doms) for i in range(doms)], "dom"),
        ([(i, (i + 4) % doms) for i in range(doms)], "dom"),
        ([(i, (i + zs) % owners) for i in range(owners)], "st"),
        ([(i, (i + 2 * zs) % owners) for i in range(owners)], "st"),
    ):
        parts.append(lax.ppermute(parts[0] if len(parts) == 1 else jnp.concatenate(parts), axis, perm))
    place = jnp.stack([me, spot // zs, spot % zs, jnp.int32(doms), jnp.int32(ys)])
    total = owners * states
    matrix = ordered(place, parts, total)
    return rotate(matrix, regrouped.reshape(total, regrouped.shape[2]))


def solution(mesh):
    sizes = (mesh.shape["dom"], mesh.shape["st"])
    return jax.shard_map(
        functools.partial(local, sizes),
        mesh=mesh,
        in_specs=(P("st", "dom", None), P("dom", None), P("st", None)),
        out_specs=P(None, ("dom", "st")),
        check_vma=False,
    )
```

```python
import functools

import jax
import jax.numpy as jnp
from jax import lax
from jax.experimental import pallas as pl
from jax.experimental.pallas import tpu as pltpu
from jax.sharding import PartitionSpec as P

DEGREE = 4
NZ = 32
LANES = 128

cheb_shift = 3.75
cheb_scale = 3.25

F32 = jnp.float32
BF16 = jnp.bfloat16

INNER_Y = LANES // NZ
RUN = NZ + 8
PLANE = INNER_Y * RUN


def one_hot(rows, cols, want):
    r = lax.broadcasted_iota(jnp.int32, (rows, cols), 0)
    c = lax.broadcasted_iota(jnp.int32, (rows, cols), 1)
    return jnp.where(c == want(r), 1.0, 0.0).astype(BF16)


def turned(block):
    eye = one_hot(LANES, LANES, lambda r: r)
    return lax.dot_general(eye, block, (((1,), (1,)), ((), ())), preferred_element_type=F32)


def stacked(rows, states, first, count):
    width = rows.shape[1]
    return jnp.concatenate(
        [
            rows[(first + p) * states : (first + p + 1) * states, j * LANES : (j + 1) * LANES]
            for p in range(count)
            for j in range(width // LANES)
        ],
        axis=0,
    )


def edges_kernel(first_ref, last_ref, pot_first_ref, pot_last_ref, low_ref, high_ref):
    states, slab, width = first_ref.shape
    rows = DEGREE * states
    pick = one_hot(rows, states * slab, lambda r: (r % states) * slab + r // states)
    first = first_ref[...].reshape(states * slab, width)
    low_ref[:rows] = jnp.dot(pick, first, preferred_element_type=F32).astype(BF16)
    low_ref[rows:] = pot_first_ref[...]
    pick = one_hot(
        rows, states * slab, lambda r: (r % states) * slab + r // states + (slab - DEGREE)
    )
    last = last_ref[...].reshape(states * slab, width)
    high_ref[:rows] = jnp.dot(pick, last, preferred_element_type=F32).astype(BF16)
    high_ref[rows:] = pot_last_ref[...]


def edges(orbitals, potential):
    states, planes, width = orbitals.shape
    slab = 8
    last = planes // slab - 1
    out = jax.ShapeDtypeStruct((DEGREE * states + slab, width), BF16)
    return pl.pallas_call(
        edges_kernel,
        grid=(1,),
        in_specs=[
            pl.BlockSpec((states, slab, width), lambda i: (0, 0, 0)),
            pl.BlockSpec((states, slab, width), lambda i: (0, last, 0)),
            pl.BlockSpec((slab, width), lambda i: (0, 0)),
            pl.BlockSpec((slab, width), lambda i: (last, 0)),
        ],
        out_specs=[pl.BlockSpec(out.shape, lambda i: (0, 0))] * 2,
        out_shape=[out, out],
        compiler_params=pltpu.CompilerParams(vmem_limit_bytes=8 << 20),
        name="edges",
    )(orbitals, orbitals, potential, potential)


def spread(pot_rows, states):
    count = pot_rows.shape[0]
    repeat = one_hot(count * states, count, lambda r: r // states)
    return jnp.dot(repeat, pot_rows, preferred_element_type=F32).astype(BF16)


def prepare_kernel(x_ref, pot_ref, field_ref, pot_out_ref):
    states, group, width = x_ref.shape
    pick = one_hot(
        states * group, states * group, lambda r: (r % states) * group + r // states
    )
    rows = x_ref[...].reshape(states * group, width)
    rows = jnp.dot(pick, rows, preferred_element_type=F32).astype(BF16)
    pot = spread(pot_ref[...], states)
    for p in range(0, group, 2):
        for source, target in ((rows, field_ref), (pot, pot_out_ref)):
            both = turned(stacked(source, states, p, 2)).astype(BF16)
            target[p] = both[:, :LANES]
            target[p + 1] = both[:, LANES:]


def prepare(orbitals, potential):
    states, planes, width = orbitals.shape
    group = 16
    out = jax.ShapeDtypeStruct((planes, LANES, LANES), BF16)
    return pl.pallas_call(
        prepare_kernel,
        grid=(planes // group,),
        in_specs=[
            pl.BlockSpec((states, group, width), lambda i: (0, i, 0)),
            pl.BlockSpec((group, width), lambda i: (i, 0)),
        ],
        out_specs=[pl.BlockSpec((group, LANES, LANES), lambda i: (i, 0, 0))] * 2,
        out_shape=[out, out],
        cost_estimate=pl.CostEstimate(
            flops=4 * 2 * states * planes * width * 256, transcendentals=0, bytes_accessed=8 << 20
        ),
        compiler_params=pltpu.CompilerParams(vmem_limit_bytes=16 << 20),
        name="prepare",
    )(orbitals, potential)


def filter_kernel(
    field_ref, pot_ref, low_ref, high_ref, out_hbm,
    even, odd, coef, done_ref, out_ref, out_sems,
):
    planes = field_ref.shape[0]
    owners, states, points = out_ref.shape
    width = LANES * (LANES // states)
    halo = DEGREE
    b = 1.0 / cheb_scale
    runs = [(r, q) for r in range(INNER_Y) for q in range(NZ // 8)]

    me, doms = lax.axis_index("dom"), lax.axis_size("dom")
    flags = (jnp.where(me > 0, 1.0, 0.0), jnp.where(me < doms - 1, 1.0, 0.0))
    def scaled(p):
        return (p - (cheb_shift - 3.0)) * 2.0

    def put(buffer, plane, values):
        for r in range(INNER_Y):
            at = pl.multiple_of(plane * PLANE + r * RUN + 8, 8)
            buffer[pl.ds(at, NZ), :] = values[r * NZ : (r + 1) * NZ]

    zero = jnp.zeros((8, LANES), F32)

    def clear(i, carry):
        for p in range(4):
            for r in range(INNER_Y):
                at = pl.multiple_of((i * 4 + p) * PLANE + r * RUN, 8)
                even[pl.ds(at, 8), :] = zero
                odd[pl.ds(at, 8), :] = zero
        return carry

    lax.fori_loop(0, (planes + 2 * halo) // 4, clear, 0)
    even[(planes + 2 * halo) * PLANE :, :] = zero
    odd[(planes + 2 * halo) * PLANE :, :] = zero

    rows = DEGREE * states
    for ref, base, at in ((low_ref, 0, 4), (high_ref, halo + planes, 0)):
        field = ref[:rows]
        pot = spread(ref[rows:], states)
        for p in range(0, halo, 2):
            both = turned(stacked(field, states, p, 2))
            put(even, base + p, both[:, :LANES])
            put(even, base + p + 1, both[:, LANES:])
            both = scaled(turned(stacked(pot, states, at + p, 2)))
            coef[base + p] = both[:, :LANES]
            coef[base + p + 1] = both[:, LANES:]

    def fill(i, carry):
        for r in range(2):
            p = i * 2 + r
            put(even, halo + p, field_ref[p].astype(F32))
            coef[halo + p] = scaled(pot_ref[p].astype(F32))
        return carry

    lax.fori_loop(0, planes // 2, fill, 0)

    lane = lax.broadcasted_iota(jnp.int32, (8, LANES), 1)
    first_y = lane < states
    last_y = lane >= LANES - states

    def step(k, plane):
        src, dst = (even, odd) if k % 2 == 1 else (odd, even)
        base = pl.multiple_of(plane * PLANE, 8)

        def rows_at(offset, r, q):
            return src[pl.ds(base + (offset + r * RUN + 8 + q * 8), 8), :]

        here = {rq: rows_at(0, *rq) for rq in runs}
        results = {}
        for r, q in runs:
            v = here[r, q]
            if r > 0:
                below = here[r - 1, q]
            else:
                below = jnp.where(first_y, 0.0, pltpu.roll(here[INNER_Y - 1, q], states, 1))
            if r < INNER_Y - 1:
                above = here[r + 1, q]
            else:
                above = jnp.where(last_y, 0.0, pltpu.roll(here[0, q], LANES - states, 1))
            along_z = rows_at(-1, r, q) + rows_at(1, r, q)
            along_x = rows_at(-PLANE, r, q) + rows_at(PLANE, r, q)
            a = coef[plane, r * NZ + q * 8 : r * NZ + q * 8 + 8, :]
            t = a * v - ((below + above) + (along_z + along_x))
            if k == 1:
                results[r, q] = (0.5 * b) * t
            else:
                results[r, q] = b * t - dst[pl.ds(base + (r * RUN + 8 + q * 8), 8), :]
        return results

    def store(k, plane, results):
        dst = odd if k % 2 == 1 else even
        base = pl.multiple_of(plane * PLANE, 8)
        for r, q in runs:
            dst[pl.ds(base + (r * RUN + 8 + q * 8), 8), :] = results[r, q]

    unroll = 8
    for k in range(1, DEGREE):
        def outer(i, carry, k=k):
            both = (k + i, halo + planes + i)
            results = [step(k, plane) for plane in both]
            for plane, flag, res in zip(both, flags, results):
                store(k, plane, {rq: v * flag for rq, v in res.items()})
            return carry

        lax.fori_loop(0, halo - k, outer, 0)

        def body(i, carry, k=k):
            results = [step(k, halo + unroll * i + r) for r in range(unroll)]
            for r in range(unroll):
                store(k, halo + unroll * i + r, results[r])
            return carry

        lax.fori_loop(0, planes // unroll, body, 0)

    per = points // width
    batch = unroll // per

    def send(i):
        return pltpu.make_async_copy(
            out_ref.at[pl.ds(i * batch, batch)], out_hbm.at[pl.ds(i * batch, batch)], out_sems.at[i]
        )

    def finish(i):
        for n in range(batch):
            at = pl.multiple_of((i * batch + n) * per * LANES, per * LANES)
            out = turned(done_ref[pl.ds(at, per * LANES), :]).astype(BF16)
            for r in range(per):
                for j in range(width // LANES):
                    out_ref[
                        i * batch + n, :, r * width + j * LANES : r * width + (j + 1) * LANES
                    ] = out[j * states : (j + 1) * states, r * LANES : (r + 1) * LANES]

    def last(i):
        for r in range(unroll):
            res = step(DEGREE, halo + unroll * i + r)
            values = jnp.concatenate([res[rq].astype(BF16) for rq in runs], axis=0)
            at = pl.multiple_of((unroll * i + r) * LANES, LANES)
            done_ref[pl.ds(at, LANES), :] = values

    def both(i, carry):
        finish(i - 1)
        last(i)
        send(i - 1).start()
        return carry

    count = planes // unroll
    last(0)
    lax.fori_loop(1, count, both, 0)
    finish(count - 1)
    send(count - 1).start()
    for i in range(count):
        send(i).wait()


def chebyshev(field, pot, low, high, owners, states):
    planes = field.shape[0]
    points = planes * LANES * LANES // states // owners
    total = planes + 2 * DEGREE
    anywhere = pl.BlockSpec(memory_space=pl.ANY)
    return pl.pallas_call(
        filter_kernel,
        in_specs=[pl.BlockSpec(memory_space=pltpu.VMEM)] * 4,
        out_specs=anywhere,
        out_shape=jax.ShapeDtypeStruct((owners, states, points), BF16),
        scratch_shapes=[
            pltpu.VMEM((total * PLANE + 8, LANES), F32),
            pltpu.VMEM((total * PLANE + 8, LANES), F32),
            pltpu.VMEM((total, LANES, LANES), F32),
            pltpu.VMEM((planes * LANES, LANES), BF16),
            pltpu.VMEM((owners, states, points), BF16),
            pltpu.SemaphoreType.DMA((planes // 8,)),
        ],
        compiler_params=pltpu.CompilerParams(vmem_limit_bytes=32 << 20),
        name="chebyshev",
    )(*in_vmem(field, pot, low, high))


def rotate_kernel(r_ref, f_ref, out_hbm, out_ref, out_sems):
    tiles = out_ref.shape[0]
    tile = out_ref.shape[2]

    def give(i):
        return pltpu.make_async_copy(
            out_ref.at[i], out_hbm.at[:, pl.ds(i * tile, tile)], out_sems.at[i]
        )

    for i in range(tiles):
        part = f_ref[:, i * tile : (i + 1) * tile]
        out_ref[i] = jnp.dot(r_ref[...], part, preferred_element_type=F32).astype(BF16)
        give(i).start()
    for i in range(tiles):
        give(i).wait()


def in_vmem(*arrays):
    return [pltpu.with_memory_space_constraint(a, pltpu.VMEM) for a in arrays]


def rotate(rotation, filtered):
    total, points = filtered.shape
    tile = 256
    tiles = points // tile
    vmem = pl.BlockSpec(memory_space=pltpu.VMEM)
    return pl.pallas_call(
        rotate_kernel,
        in_specs=[vmem, vmem],
        out_specs=pl.BlockSpec(memory_space=pl.ANY),
        out_shape=jax.ShapeDtypeStruct((rotation.shape[0], points), BF16),
        scratch_shapes=[
            pltpu.VMEM((tiles, rotation.shape[0], tile), BF16),
            pltpu.SemaphoreType.DMA((tiles,)),
        ],
        compiler_params=pltpu.CompilerParams(vmem_limit_bytes=12 << 20),
        name="rotate",
    )(*in_vmem(rotation, filtered))


def order_kernel(place_ref, *refs):
    *parts, out_ref = refs
    dom, y, z = place_ref[0], place_ref[1], place_ref[2]
    doms, ys = place_ref[3], place_ref[4]
    total, cols = out_ref.shape
    own = parts[0].shape[0]
    r = lax.broadcasted_iota(jnp.int32, (8, total), 1) // own

    def bit(n):
        return (r >> n) & 1

    source = ((dom + 2 * doms - 4 * bit(2) - 2 * bit(1)) & (doms - 1)) ^ bit(0)
    zs = (z + doms - source) & (doms - 1)
    y_source = (y + 2 * ys - bit(3) - 2 * bit(4)) & (ys - 1)
    want = (y_source * doms + zs) * own
    want = want + lax.broadcasted_iota(jnp.int32, (8, total), 1) % own
    rows = lax.broadcasted_iota(jnp.int32, (total, total), 0)
    pick = jnp.where(rows == jnp.broadcast_to(want[:1], (total, total)), 1.0, 0.0).astype(BF16)
    gathered = jnp.concatenate([p[...] for p in parts], axis=0)
    out_ref[...] = jnp.dot(pick, gathered, preferred_element_type=F32).astype(BF16)


def ordered(place, parts, total):
    vmem = pl.BlockSpec(memory_space=pltpu.VMEM)
    cols = parts[0].shape[1]
    return pl.pallas_call(
        order_kernel,
        in_specs=[pl.BlockSpec(memory_space=pltpu.SMEM)] + [vmem] * len(parts),
        out_specs=vmem,
        out_shape=jax.ShapeDtypeStruct((total, cols), BF16),
        compiler_params=pltpu.CompilerParams(vmem_limit_bytes=8 << 20),
        name="order",
    )(place, *parts)


def local(sizes, orbitals, potential, rotation):
    doms, owners = sizes
    zs = doms
    ys = owners // zs
    states = orbitals.shape[0]
    me, spot = lax.axis_index("dom"), lax.axis_index("st")
    up = [(i, i + 1) for i in range(doms - 1)]
    down = [(i + 1, i) for i in range(doms - 1)]
    orbitals = pltpu.with_memory_space_constraint(orbitals, pltpu.HBM)
    potential = pltpu.with_memory_space_constraint(potential, pltpu.HBM)
    low_send, high_send = edges(orbitals, potential)
    low = lax.ppermute(high_send, "dom", up)
    high = lax.ppermute(low_send, "dom", down)
    shift = [
        (d * owners + y * zs + z, d * owners + y * zs + (z + d) % zs)
        for d in range(doms)
        for y in range(ys)
        for z in range(zs)
    ]
    rotation, low_send = lax.optimization_barrier((rotation, low_send))
    rows = lax.ppermute(rotation, ("dom", "st"), shift)
    field, pot = prepare(orbitals, potential)
    rows, field = lax.optimization_barrier((rows, field))
    filtered = chebyshev(field, pot, low, high, owners, states)
    rows, _ = lax.optimization_barrier((rows, filtered))
    regrouped = lax.all_to_all(filtered, "st", split_axis=0, concat_axis=0, tiled=True)
    parts = [rows]
    swap = [(i, i ^ 1) for i in range(doms)]
    for perm, axis in (
        (swap, "dom"),
        ([(i, (i + 2) % doms) for i in range(doms)], "dom"),
        ([(i, (i + 4) % doms) for i in range(doms)], "dom"),
        ([(i, (i + zs) % owners) for i in range(owners)], "st"),
        ([(i, (i + 2 * zs) % owners) for i in range(owners)], "st"),
    ):
        parts.append(lax.ppermute(parts[0] if len(parts) == 1 else jnp.concatenate(parts), axis, perm))
    place = jnp.stack([me, spot // zs, spot % zs, jnp.int32(doms), jnp.int32(ys)])
    total = owners * states
    matrix = ordered(place, parts, total)
    return rotate(matrix, regrouped.reshape(total, regrouped.shape[2]))


def solution(mesh):
    sizes = (mesh.shape["dom"], mesh.shape["st"])
    return jax.shard_map(
        functools.partial(local, sizes),
        mesh=mesh,
        in_specs=(P("st", "dom", None), P("dom", None), P("st", None)),
        out_specs=P(None, ("dom", "st")),
        check_vma=False,
    )
```

```python
import functools

import jax
import jax.numpy as jnp
from jax import lax
from jax.experimental import pallas as pl
from jax.experimental.pallas import tpu as pltpu
from jax.sharding import PartitionSpec as P

DEGREE = 4
NZ = 32
LANES = 128

cheb_shift = 3.75
cheb_scale = 3.25

F32 = jnp.float32
BF16 = jnp.bfloat16

INNER_Y = LANES // NZ
RUN = NZ + 8
PLANE = INNER_Y * RUN


def one_hot(rows, cols, want):
    r = lax.broadcasted_iota(jnp.int32, (rows, cols), 0)
    c = lax.broadcasted_iota(jnp.int32, (rows, cols), 1)
    return jnp.where(c == want(r), 1.0, 0.0).astype(BF16)


def turned(block):
    eye = one_hot(LANES, LANES, lambda r: r)
    return lax.dot_general(eye, block, (((1,), (1,)), ((), ())), preferred_element_type=F32)


def stacked(rows, states, first, count):
    width = rows.shape[1]
    return jnp.concatenate(
        [
            rows[(first + p) * states : (first + p + 1) * states, j * LANES : (j + 1) * LANES]
            for p in range(count)
            for j in range(width // LANES)
        ],
        axis=0,
    )


def edges_kernel(first_ref, last_ref, pot_first_ref, pot_last_ref, low_ref, high_ref):
    states, slab, width = first_ref.shape
    rows = DEGREE * states
    pick = one_hot(rows, states * slab, lambda r: (r % states) * slab + r // states)
    first = first_ref[...].reshape(states * slab, width)
    low_ref[:rows] = jnp.dot(pick, first, preferred_element_type=F32).astype(BF16)
    low_ref[rows:] = pot_first_ref[...]
    pick = one_hot(
        rows, states * slab, lambda r: (r % states) * slab + r // states + (slab - DEGREE)
    )
    last = last_ref[...].reshape(states * slab, width)
    high_ref[:rows] = jnp.dot(pick, last, preferred_element_type=F32).astype(BF16)
    high_ref[rows:] = pot_last_ref[...]


def edges(orbitals, potential):
    states, planes, width = orbitals.shape
    slab = 8
    last = planes // slab - 1
    out = jax.ShapeDtypeStruct((DEGREE * states + slab, width), BF16)
    return pl.pallas_call(
        edges_kernel,
        grid=(1,),
        in_specs=[
            pl.BlockSpec((states, slab, width), lambda i: (0, 0, 0)),
            pl.BlockSpec((states, slab, width), lambda i: (0, last, 0)),
            pl.BlockSpec((slab, width), lambda i: (0, 0)),
            pl.BlockSpec((slab, width), lambda i: (last, 0)),
        ],
        out_specs=[pl.BlockSpec(out.shape, lambda i: (0, 0))] * 2,
        out_shape=[out, out],
        compiler_params=pltpu.CompilerParams(vmem_limit_bytes=8 << 20),
        name="edges",
    )(orbitals, orbitals, potential, potential)


def spread(pot_rows, states):
    count = pot_rows.shape[0]
    repeat = one_hot(count * states, count, lambda r: r // states)
    return jnp.dot(repeat, pot_rows, preferred_element_type=F32).astype(BF16)


def prepare_kernel(x_ref, pot_ref, field_ref, pot_out_ref, select):
    states, group, width = x_ref.shape
    tiles = width // LANES

    @pl.when(pl.program_id(0) == 0)
    def _():
        r = lax.broadcasted_iota(jnp.int32, select.shape, 0)
        col = lax.broadcasted_iota(jnp.int32, select.shape, 1)
        want = (col % LANES) // states * group + col // LANES
        select[...] = jnp.where(r == want, 1.0, 0.0).astype(BF16)

    pick = one_hot(
        states * group, states * group, lambda r: (r % states) * group + r // states
    )
    rows = x_ref[...].reshape(states * group, width)
    pot = jnp.concatenate(
        [pot_ref[:, j * LANES : (j + 1) * LANES] for j in range(tiles)], axis=0
    )
    pot = turned(pot).astype(BF16)
    rows = jnp.dot(pick, rows, preferred_element_type=F32).astype(BF16)
    for p in range(0, group, 2):
        at = slice(p * LANES, (p + 2) * LANES)
        spreads = jnp.dot(pot, select[:, at], preferred_element_type=F32).astype(BF16)
        both = turned(stacked(rows, states, p, 2)).astype(BF16)
        for source, target in ((both, field_ref), (spreads, pot_out_ref)):
            target[p] = source[:, :LANES]
            target[p + 1] = source[:, LANES:]


def prepare(orbitals, potential):
    states, planes, width = orbitals.shape
    group = 16
    out = jax.ShapeDtypeStruct((planes, LANES, LANES), BF16)
    return pl.pallas_call(
        prepare_kernel,
        grid=(planes // group,),
        in_specs=[
            pl.BlockSpec((states, group, width), lambda i: (0, i, 0)),
            pl.BlockSpec((group, width), lambda i: (i, 0)),
        ],
        out_specs=[pl.BlockSpec((group, LANES, LANES), lambda i: (i, 0, 0))] * 2,
        out_shape=[out, out],
        scratch_shapes=[pltpu.VMEM((group * width // LANES, group * LANES), BF16)],
        cost_estimate=pl.CostEstimate(
            flops=4 * 2 * states * planes * width * 256, transcendentals=0, bytes_accessed=8 << 20
        ),
        compiler_params=pltpu.CompilerParams(vmem_limit_bytes=16 << 20),
        name="prepare",
    )(orbitals, potential)


def filter_kernel(
    field_ref, pot_ref, low_ref, high_ref, out_hbm,
    even, odd, coef, done_ref, out_ref, out_sems,
):
    planes = field_ref.shape[0]
    owners, states, points = out_ref.shape
    width = LANES * (LANES // states)
    halo = DEGREE
    b = 1.0 / cheb_scale
    runs = [(r, q) for r in range(INNER_Y) for q in range(NZ // 8)]

    me, doms = lax.axis_index("dom"), lax.axis_size("dom")
    flags = (jnp.where(me > 0, 1.0, 0.0), jnp.where(me < doms - 1, 1.0, 0.0))
    def scaled(p):
        return (p - (cheb_shift - 3.0)) * 2.0

    def put(buffer, plane, values):
        for r in range(INNER_Y):
            at = pl.multiple_of(plane * PLANE + r * RUN + 8, 8)
            buffer[pl.ds(at, NZ), :] = values[r * NZ : (r + 1) * NZ]

    zero = jnp.zeros((8, LANES), F32)

    def clear(i, carry):
        for p in range(4):
            for r in range(INNER_Y):
                at = pl.multiple_of((i * 4 + p) * PLANE + r * RUN, 8)
                even[pl.ds(at, 8), :] = zero
                odd[pl.ds(at, 8), :] = zero
        return carry

    lax.fori_loop(0, (planes + 2 * halo) // 4, clear, 0)
    even[(planes + 2 * halo) * PLANE :, :] = zero
    odd[(planes + 2 * halo) * PLANE :, :] = zero

    rows = DEGREE * states
    for ref, base, at in ((low_ref, 0, 4), (high_ref, halo + planes, 0)):
        field = ref[:rows]
        pot = spread(ref[rows:], states)
        for p in range(0, halo, 2):
            both = turned(stacked(field, states, p, 2))
            put(even, base + p, both[:, :LANES])
            put(even, base + p + 1, both[:, LANES:])
            both = scaled(turned(stacked(pot, states, at + p, 2)))
            coef[base + p] = both[:, :LANES]
            coef[base + p + 1] = both[:, LANES:]

    for p in range(planes):
        put(even, halo + p, field_ref[p].astype(F32))
        coef[halo + p] = scaled(pot_ref[p].astype(F32))

    lane = lax.broadcasted_iota(jnp.int32, (8, LANES), 1)
    first_y = lane < states
    last_y = lane >= LANES - states

    def step(k, plane):
        src, dst = (even, odd) if k % 2 == 1 else (odd, even)
        base = pl.multiple_of(plane * PLANE, 8)

        def rows_at(offset, r, q):
            return src[pl.ds(base + (offset + r * RUN + 8 + q * 8), 8), :]

        here = {rq: rows_at(0, *rq) for rq in runs}
        results = {}
        for r, q in runs:
            v = here[r, q]
            if r > 0:
                below = here[r - 1, q]
            else:
                below = jnp.where(first_y, 0.0, pltpu.roll(here[INNER_Y - 1, q], states, 1))
            if r < INNER_Y - 1:
                above = here[r + 1, q]
            else:
                above = jnp.where(last_y, 0.0, pltpu.roll(here[0, q], LANES - states, 1))
            along_z = rows_at(-1, r, q) + rows_at(1, r, q)
            along_x = rows_at(-PLANE, r, q) + rows_at(PLANE, r, q)
            a = coef[plane, r * NZ + q * 8 : r * NZ + q * 8 + 8, :]
            t = a * v - ((below + above) + (along_z + along_x))
            if k == 1:
                results[r, q] = (0.5 * b) * t
            else:
                results[r, q] = b * t - dst[pl.ds(base + (r * RUN + 8 + q * 8), 8), :]
        return results

    def store(k, plane, results):
        dst = odd if k % 2 == 1 else even
        base = pl.multiple_of(plane * PLANE, 8)
        for r, q in runs:
            dst[pl.ds(base + (r * RUN + 8 + q * 8), 8), :] = results[r, q]

    unroll = 8
    for k in range(1, DEGREE):
        def outer(i, carry, k=k):
            both = (k + i, halo + planes + i)
            results = [step(k, plane) for plane in both]
            for plane, flag, res in zip(both, flags, results):
                store(k, plane, {rq: v * flag for rq, v in res.items()})
            return carry

        lax.fori_loop(0, halo - k, outer, 0)

        def body(i, carry, k=k):
            results = [step(k, halo + unroll * i + r) for r in range(unroll)]
            for r in range(unroll):
                store(k, halo + unroll * i + r, results[r])
            return carry

        lax.fori_loop(0, planes // unroll, body, 0)

    per = points // width
    batch = unroll // per

    def send(i):
        return pltpu.make_async_copy(
            out_ref.at[pl.ds(i * batch, batch)], out_hbm.at[pl.ds(i * batch, batch)], out_sems.at[i]
        )

    def finish(i):
        for n in range(batch):
            at = pl.multiple_of((i * batch + n) * per * LANES, per * LANES)
            out = turned(done_ref[pl.ds(at, per * LANES), :]).astype(BF16)
            for r in range(per):
                for j in range(width // LANES):
                    out_ref[
                        i * batch + n, :, r * width + j * LANES : r * width + (j + 1) * LANES
                    ] = out[j * states : (j + 1) * states, r * LANES : (r + 1) * LANES]

    def last(i):
        for r in range(unroll):
            res = step(DEGREE, halo + unroll * i + r)
            values = jnp.concatenate([res[rq].astype(BF16) for rq in runs], axis=0)
            at = pl.multiple_of((unroll * i + r) * LANES, LANES)
            done_ref[pl.ds(at, LANES), :] = values

    def both(i, carry):
        finish(i - 1)
        last(i)
        send(i - 1).start()
        return carry

    count = planes // unroll
    last(0)
    lax.fori_loop(1, count, both, 0)
    finish(count - 1)
    send(count - 1).start()
    for i in range(count):
        send(i).wait()


def chebyshev(field, pot, low, high, owners, states):
    planes = field.shape[0]
    points = planes * LANES * LANES // states // owners
    total = planes + 2 * DEGREE
    anywhere = pl.BlockSpec(memory_space=pl.ANY)
    return pl.pallas_call(
        filter_kernel,
        in_specs=[pl.BlockSpec(memory_space=pltpu.VMEM)] * 4,
        out_specs=anywhere,
        out_shape=jax.ShapeDtypeStruct((owners, states, points), BF16),
        scratch_shapes=[
            pltpu.VMEM((total * PLANE + 8, LANES), F32),
            pltpu.VMEM((total * PLANE + 8, LANES), F32),
            pltpu.VMEM((total, LANES, LANES), F32),
            pltpu.VMEM((planes * LANES, LANES), BF16),
            pltpu.VMEM((owners, states, points), BF16),
            pltpu.SemaphoreType.DMA((planes // 8,)),
        ],
        compiler_params=pltpu.CompilerParams(vmem_limit_bytes=32 << 20),
        name="chebyshev",
    )(*in_vmem(field, pot, low, high))


def rotate_kernel(r_ref, f_ref, out_hbm, out_ref, out_sems):
    tiles = out_ref.shape[0]
    tile = out_ref.shape[2]

    def give(i):
        return pltpu.make_async_copy(
            out_ref.at[i], out_hbm.at[:, pl.ds(i * tile, tile)], out_sems.at[i]
        )

    for i in range(tiles):
        part = f_ref[:, i * tile : (i + 1) * tile]
        out_ref[i] = jnp.dot(r_ref[...], part, preferred_element_type=F32).astype(BF16)
        give(i).start()
    for i in range(tiles):
        give(i).wait()


def in_vmem(*arrays):
    return [pltpu.with_memory_space_constraint(a, pltpu.VMEM) for a in arrays]


def rotate(rotation, filtered):
    total, points = filtered.shape
    tile = 256
    tiles = points // tile
    vmem = pl.BlockSpec(memory_space=pltpu.VMEM)
    return pl.pallas_call(
        rotate_kernel,
        in_specs=[vmem, vmem],
        out_specs=pl.BlockSpec(memory_space=pl.ANY),
        out_shape=jax.ShapeDtypeStruct((rotation.shape[0], points), BF16),
        scratch_shapes=[
            pltpu.VMEM((tiles, rotation.shape[0], tile), BF16),
            pltpu.SemaphoreType.DMA((tiles,)),
        ],
        compiler_params=pltpu.CompilerParams(vmem_limit_bytes=12 << 20),
        name="rotate",
    )(*in_vmem(rotation, filtered))


def order_kernel(place_ref, *refs):
    *parts, out_ref = refs
    dom, y, z = place_ref[0], place_ref[1], place_ref[2]
    doms, ys = place_ref[3], place_ref[4]
    total, cols = out_ref.shape
    own = parts[0].shape[0]
    r = lax.broadcasted_iota(jnp.int32, (8, total), 1) // own

    def bit(n):
        return (r >> n) & 1

    source = ((dom + 2 * doms - 4 * bit(2) - 2 * bit(1)) & (doms - 1)) ^ bit(0)
    zs = (z + doms - source) & (doms - 1)
    y_source = (y + 2 * ys - bit(3) - 2 * bit(4)) & (ys - 1)
    want = (y_source * doms + zs) * own
    want = want + lax.broadcasted_iota(jnp.int32, (8, total), 1) % own
    rows = lax.broadcasted_iota(jnp.int32, (total, total), 0)
    pick = jnp.where(rows == jnp.broadcast_to(want[:1], (total, total)), 1.0, 0.0).astype(BF16)
    gathered = jnp.concatenate([p[...] for p in parts], axis=0)
    out_ref[...] = jnp.dot(pick, gathered, preferred_element_type=F32).astype(BF16)


def ordered(place, parts, total):
    vmem = pl.BlockSpec(memory_space=pltpu.VMEM)
    cols = parts[0].shape[1]
    return pl.pallas_call(
        order_kernel,
        in_specs=[pl.BlockSpec(memory_space=pltpu.SMEM)] + [vmem] * len(parts),
        out_specs=vmem,
        out_shape=jax.ShapeDtypeStruct((total, cols), BF16),
        compiler_params=pltpu.CompilerParams(vmem_limit_bytes=8 << 20),
        name="order",
    )(place, *parts)


def local(sizes, orbitals, potential, rotation):
    doms, owners = sizes
    zs = doms
    ys = owners // zs
    states = orbitals.shape[0]
    me, spot = lax.axis_index("dom"), lax.axis_index("st")
    up = [(i, i + 1) for i in range(doms - 1)]
    down = [(i + 1, i) for i in range(doms - 1)]
    low_send, high_send = edges(
        pltpu.with_memory_space_constraint(orbitals, pltpu.HBM),
        pltpu.with_memory_space_constraint(potential, pltpu.HBM),
    )
    low = lax.ppermute(high_send, "dom", up)
    high = lax.ppermute(low_send, "dom", down)
    shift = [
        (d * owners + y * zs + z, d * owners + y * zs + (z + d) % zs)
        for d in range(doms)
        for y in range(ys)
        for z in range(zs)
    ]
    rotation, low_send = lax.optimization_barrier((rotation, low_send))
    rows = lax.ppermute(rotation, ("dom", "st"), shift)
    field, pot = prepare(orbitals, potential)
    rows, field = lax.optimization_barrier((rows, field))
    filtered = chebyshev(field, pot, low, high, owners, states)
    rows, _ = lax.optimization_barrier((rows, filtered))
    regrouped = lax.all_to_all(filtered, "st", split_axis=0, concat_axis=0, tiled=True)
    parts = [rows]
    swap = [(i, i ^ 1) for i in range(doms)]
    for perm, axis in (
        (swap, "dom"),
        ([(i, (i + 2) % doms) for i in range(doms)], "dom"),
        ([(i, (i + 4) % doms) for i in range(doms)], "dom"),
        ([(i, (i + zs) % owners) for i in range(owners)], "st"),
        ([(i, (i + 2 * zs) % owners) for i in range(owners)], "st"),
    ):
        parts.append(lax.ppermute(parts[0] if len(parts) == 1 else jnp.concatenate(parts), axis, perm))
    place = jnp.stack([me, spot // zs, spot % zs, jnp.int32(doms), jnp.int32(ys)])
    total = owners * states
    matrix = ordered(place, parts, total)
    return rotate(matrix, regrouped.reshape(total, regrouped.shape[2]))


def solution(mesh):
    sizes = (mesh.shape["dom"], mesh.shape["st"])
    return jax.shard_map(
        functools.partial(local, sizes),
        mesh=mesh,
        in_specs=(P("st", "dom", None), P("dom", None), P("st", None)),
        out_specs=P(None, ("dom", "st")),
        check_vma=False,
    )
```

```python
import functools

import jax
import jax.numpy as jnp
from jax import lax
from jax.experimental import pallas as pl
from jax.experimental.pallas import tpu as pltpu
from jax.sharding import PartitionSpec as P

DEGREE = 4
NZ = 32
LANES = 128

cheb_shift = 3.75
cheb_scale = 3.25

F32 = jnp.float32
BF16 = jnp.bfloat16

INNER_Y = LANES // NZ
RUN = NZ + 8
PLANE = INNER_Y * RUN


def one_hot(rows, cols, want):
    r = lax.broadcasted_iota(jnp.int32, (rows, cols), 0)
    c = lax.broadcasted_iota(jnp.int32, (rows, cols), 1)
    return jnp.where(c == want(r), 1.0, 0.0).astype(BF16)


def turned(block):
    eye = one_hot(LANES, LANES, lambda r: r)
    return lax.dot_general(eye, block, (((1,), (1,)), ((), ())), preferred_element_type=F32)


def stacked(rows, states, first, count):
    width = rows.shape[1]
    return jnp.concatenate(
        [
            rows[(first + p) * states : (first + p + 1) * states, j * LANES : (j + 1) * LANES]
            for p in range(count)
            for j in range(width // LANES)
        ],
        axis=0,
    )


def edges_kernel(first_ref, last_ref, pot_first_ref, pot_last_ref, low_ref, high_ref):
    states, slab, width = first_ref.shape
    rows = DEGREE * states
    pick = one_hot(rows, states * slab, lambda r: (r % states) * slab + r // states)
    first = first_ref[...].reshape(states * slab, width)
    low_ref[:rows] = jnp.dot(pick, first, preferred_element_type=F32).astype(BF16)
    low_ref[rows:] = pot_first_ref[...]
    pick = one_hot(
        rows, states * slab, lambda r: (r % states) * slab + r // states + (slab - DEGREE)
    )
    last = last_ref[...].reshape(states * slab, width)
    high_ref[:rows] = jnp.dot(pick, last, preferred_element_type=F32).astype(BF16)
    high_ref[rows:] = pot_last_ref[...]


def edges(orbitals, potential):
    states, planes, width = orbitals.shape
    slab = 8
    last = planes // slab - 1
    out = jax.ShapeDtypeStruct((DEGREE * states + slab, width), BF16)
    return pl.pallas_call(
        edges_kernel,
        grid=(1,),
        in_specs=[
            pl.BlockSpec((states, slab, width), lambda i: (0, 0, 0)),
            pl.BlockSpec((states, slab, width), lambda i: (0, last, 0)),
            pl.BlockSpec((slab, width), lambda i: (0, 0)),
            pl.BlockSpec((slab, width), lambda i: (last, 0)),
        ],
        out_specs=[pl.BlockSpec(out.shape, lambda i: (0, 0))] * 2,
        out_shape=[out, out],
        compiler_params=pltpu.CompilerParams(vmem_limit_bytes=8 << 20),
        name="edges",
    )(orbitals, orbitals, potential, potential)


def spread(pot_rows, states):
    count = pot_rows.shape[0]
    repeat = one_hot(count * states, count, lambda r: r // states)
    return jnp.dot(repeat, pot_rows, preferred_element_type=F32).astype(BF16)


def prepare_kernel(x_ref, pot_ref, field_ref, pot_out_ref, select):
    states, group, width = x_ref.shape
    tiles = width // LANES

    @pl.when(pl.program_id(0) == 0)
    def _():
        r = lax.broadcasted_iota(jnp.int32, select.shape, 0)
        col = lax.broadcasted_iota(jnp.int32, select.shape, 1)
        want = (col % LANES) // states * group + col // LANES
        select[...] = jnp.where(r == want, 1.0, 0.0).astype(BF16)

    pick = one_hot(
        states * group, states * group, lambda r: (r % states) * group + r // states
    )
    rows = x_ref[...].reshape(states * group, width)
    pot = jnp.concatenate(
        [pot_ref[:, j * LANES : (j + 1) * LANES] for j in range(tiles)], axis=0
    )
    pot = turned(pot).astype(BF16)
    rows = jnp.dot(pick, rows, preferred_element_type=F32).astype(BF16)
    for p in range(0, group, 2):
        at = slice(p * LANES, (p + 2) * LANES)
        spreads = jnp.dot(pot, select[:, at], preferred_element_type=F32).astype(BF16)
        both = turned(stacked(rows, states, p, 2)).astype(BF16)
        for source, target in ((both, field_ref), (spreads, pot_out_ref)):
            target[p] = source[:, :LANES]
            target[p + 1] = source[:, LANES:]


def prepare(orbitals, potential):
    states, planes, width = orbitals.shape
    group = 16
    out = jax.ShapeDtypeStruct((planes, LANES, LANES), BF16)
    return pl.pallas_call(
        prepare_kernel,
        grid=(planes // group,),
        in_specs=[
            pl.BlockSpec((states, group, width), lambda i: (0, i, 0)),
            pl.BlockSpec((group, width), lambda i: (i, 0)),
        ],
        out_specs=[pl.BlockSpec((group, LANES, LANES), lambda i: (i, 0, 0))] * 2,
        out_shape=[out, out],
        scratch_shapes=[pltpu.VMEM((group * width // LANES, group * LANES), BF16)],
        cost_estimate=pl.CostEstimate(
            flops=4 * 2 * states * planes * width * 256, transcendentals=0, bytes_accessed=8 << 20
        ),
        compiler_params=pltpu.CompilerParams(vmem_limit_bytes=16 << 20),
        name="prepare",
    )(orbitals, potential)


def filter_kernel(
    field_ref, pot_ref, low_ref, high_ref, out_hbm,
    even, odd, coef, done_ref, out_ref, out_sems,
):
    planes = field_ref.shape[0]
    owners, states, points = out_ref.shape
    width = LANES * (LANES // states)
    halo = DEGREE
    b = 1.0 / cheb_scale

    me, doms = lax.axis_index("dom"), lax.axis_size("dom")
    flags = (jnp.where(me > 0, 1.0, 0.0), jnp.where(me < doms - 1, 1.0, 0.0))
    def scaled(p):
        return (p - (cheb_shift - 3.0)) * 2.0

    def put(buffer, plane, values):
        for r in range(INNER_Y):
            at = pl.multiple_of(plane * PLANE + r * RUN + 8, 8)
            buffer[pl.ds(at, NZ), :] = values[r * NZ : (r + 1) * NZ]

    zero = jnp.zeros((8, LANES), F32)

    def clear(i, carry):
        for p in range(4):
            for r in range(INNER_Y):
                at = pl.multiple_of((i * 4 + p) * PLANE + r * RUN, 8)
                even[pl.ds(at, 8), :] = zero
                odd[pl.ds(at, 8), :] = zero
        return carry

    lax.fori_loop(0, (planes + 2 * halo) // 4, clear, 0)
    even[(planes + 2 * halo) * PLANE :, :] = zero
    odd[(planes + 2 * halo) * PLANE :, :] = zero

    rows = DEGREE * states
    for ref, base, at in ((low_ref, 0, 4), (high_ref, halo + planes, 0)):
        field = ref[:rows]
        pot = spread(ref[rows:], states)
        for p in range(0, halo, 2):
            both = turned(stacked(field, states, p, 2))
            put(even, base + p, both[:, :LANES])
            put(even, base + p + 1, both[:, LANES:])
            both = scaled(turned(stacked(pot, states, at + p, 2)))
            coef[base + p] = both[:, :LANES]
            coef[base + p + 1] = both[:, LANES:]

    for p in range(planes):
        put(even, halo + p, field_ref[p].astype(F32))
        coef[halo + p] = scaled(pot_ref[p].astype(F32))

    lane = lax.broadcasted_iota(jnp.int32, (8, LANES), 1)
    first_y = lane < states
    last_y = lane >= LANES - states

    def sweep(k, first, count, together, emit):
        src, dst = (even, odd) if k % 2 == 1 else (odd, even)
        base = pl.multiple_of(first * PLANE, 8)
        for start in range(0, NZ // 8, together):
            cols = range(start, start + together)

            def rows_at(n, r, q, offset=0):
                return src[pl.ds(base + (n * PLANE + r * RUN + 8 + q * 8 + offset), 8), :]

            def column(n):
                return {(r, q): rows_at(n, r, q) for q in cols for r in range(INNER_Y)}

            before, here = column(-1), column(0)
            for n in range(count):
                after = column(n + 1)
                for r in range(INNER_Y):
                    values = []
                    for q in cols:
                        v = here[r, q]
                        if r > 0:
                            below = here[r - 1, q]
                        else:
                            below = pltpu.roll(here[INNER_Y - 1, q], states, 1)
                            below = jnp.where(first_y, 0.0, below)
                        if r < INNER_Y - 1:
                            above = here[r + 1, q]
                        else:
                            above = pltpu.roll(here[0, q], LANES - states, 1)
                            above = jnp.where(last_y, 0.0, above)
                        along_z = rows_at(n, r, q, -1) + rows_at(n, r, q, 1)
                        along_x = before[r, q] + after[r, q]
                        at = r * NZ + q * 8
                        t = coef[first + n, at : at + 8, :] * v
                        t = t - ((below + above) + (along_z + along_x))
                        if k == 1:
                            values.append((0.5 * b) * t)
                        else:
                            at = base + (n * PLANE + r * RUN + 8 + q * 8)
                            values.append(b * t - dst[pl.ds(at, 8), :])
                    emit(n, r, start, values)
                before, here = here, after

    def store(k, first, flag=None):
        dst = odd if k % 2 == 1 else even
        base = pl.multiple_of(first * PLANE, 8)

        def emit(n, r, q, values):
            for i, v in enumerate(values):
                at = base + (n * PLANE + r * RUN + 8 + (q + i) * 8)
                dst[pl.ds(at, 8), :] = v if flag is None else v * flag

        return emit

    unroll = 8
    for k in range(1, DEGREE):
        def outer(i, carry, k=k):
            for plane, flag in zip((k + i, halo + planes + i), flags):
                sweep(k, plane, 1, 1, store(k, plane, flag))
            return carry

        lax.fori_loop(0, halo - k, outer, 0)

        def body(i, carry, k=k):
            first = halo + unroll * i
            sweep(k, first, unroll, 1, store(k, first))
            return carry

        lax.fori_loop(0, planes // unroll, body, 0)

    per = points // width
    batch = unroll // per

    def send(i):
        return pltpu.make_async_copy(
            out_ref.at[pl.ds(i * batch, batch)], out_hbm.at[pl.ds(i * batch, batch)], out_sems.at[i]
        )

    def finish(i):
        for n in range(batch):
            at = pl.multiple_of((i * batch + n) * per * LANES, per * LANES)
            out = turned(done_ref[pl.ds(at, per * LANES), :]).astype(BF16)
            for r in range(per):
                for j in range(width // LANES):
                    out_ref[
                        i * batch + n, :, r * width + j * LANES : r * width + (j + 1) * LANES
                    ] = out[j * states : (j + 1) * states, r * LANES : (r + 1) * LANES]

    def last(i):
        def emit(n, r, q, values):
            at = pl.multiple_of((unroll * i + n) * LANES + r * NZ + q * 8, 16)
            done_ref[pl.ds(at, 16), :] = jnp.concatenate(values, axis=0).astype(BF16)

        sweep(DEGREE, halo + unroll * i, unroll, 2, emit)

    def both(i, carry):
        finish(i - 1)
        last(i)
        send(i - 1).start()
        return carry

    count = planes // unroll
    last(0)
    lax.fori_loop(1, count, both, 0)
    finish(count - 1)
    send(count - 1).start()
    for i in range(count):
        send(i).wait()


def chebyshev(field, pot, low, high, owners, states):
    planes = field.shape[0]
    points = planes * LANES * LANES // states // owners
    total = planes + 2 * DEGREE
    anywhere = pl.BlockSpec(memory_space=pl.ANY)
    return pl.pallas_call(
        filter_kernel,
        in_specs=[pl.BlockSpec(memory_space=pltpu.VMEM)] * 4,
        out_specs=anywhere,
        out_shape=jax.ShapeDtypeStruct((owners, states, points), BF16),
        scratch_shapes=[
            pltpu.VMEM((total * PLANE + 8, LANES), F32),
            pltpu.VMEM((total * PLANE + 8, LANES), F32),
            pltpu.VMEM((total, LANES, LANES), F32),
            pltpu.VMEM((planes * LANES, LANES), BF16),
            pltpu.VMEM((owners, states, points), BF16),
            pltpu.SemaphoreType.DMA((planes // 8,)),
        ],
        compiler_params=pltpu.CompilerParams(vmem_limit_bytes=32 << 20),
        name="chebyshev",
    )(*in_vmem(field, pot, low, high))


def rotate_kernel(r_ref, f_ref, out_hbm, out_ref, out_sems):
    tiles = out_ref.shape[0]
    tile = out_ref.shape[2]

    def give(i):
        return pltpu.make_async_copy(
            out_ref.at[i], out_hbm.at[:, pl.ds(i * tile, tile)], out_sems.at[i]
        )

    for i in range(tiles):
        part = f_ref[:, i * tile : (i + 1) * tile]
        out_ref[i] = jnp.dot(r_ref[...], part, preferred_element_type=F32).astype(BF16)
        give(i).start()
    for i in range(tiles):
        give(i).wait()


def in_vmem(*arrays):
    return [pltpu.with_memory_space_constraint(a, pltpu.VMEM) for a in arrays]


def rotate(rotation, filtered):
    total, points = filtered.shape
    tile = 256
    tiles = points // tile
    vmem = pl.BlockSpec(memory_space=pltpu.VMEM)
    return pl.pallas_call(
        rotate_kernel,
        in_specs=[vmem, vmem],
        out_specs=pl.BlockSpec(memory_space=pl.ANY),
        out_shape=jax.ShapeDtypeStruct((rotation.shape[0], points), BF16),
        scratch_shapes=[
            pltpu.VMEM((tiles, rotation.shape[0], tile), BF16),
            pltpu.SemaphoreType.DMA((tiles,)),
        ],
        compiler_params=pltpu.CompilerParams(vmem_limit_bytes=12 << 20),
        name="rotate",
    )(*in_vmem(rotation, filtered))


def order_kernel(place_ref, *refs):
    *parts, out_ref = refs
    dom, y, z = place_ref[0], place_ref[1], place_ref[2]
    doms, ys = place_ref[3], place_ref[4]
    total, cols = out_ref.shape
    own = parts[0].shape[0]
    r = lax.broadcasted_iota(jnp.int32, (8, total), 1) // own

    def bit(n):
        return (r >> n) & 1

    source = ((dom + 2 * doms - 4 * bit(4) - 2 * bit(3)) & (doms - 1)) ^ bit(2)
    zs = (z + doms - source) & (doms - 1)
    y_source = (y + 2 * ys - bit(0) - 2 * bit(1)) & (ys - 1)
    want = (y_source * doms + zs) * own
    want = want + lax.broadcasted_iota(jnp.int32, (8, total), 1) % own
    rows = lax.broadcasted_iota(jnp.int32, (total, total), 0)
    pick = jnp.where(rows == jnp.broadcast_to(want[:1], (total, total)), 1.0, 0.0).astype(BF16)
    gathered = jnp.concatenate([p[...] for p in parts], axis=0)
    out_ref[...] = jnp.dot(pick, gathered, preferred_element_type=F32).astype(BF16)


def ordered(place, parts, total):
    vmem = pl.BlockSpec(memory_space=pltpu.VMEM)
    cols = parts[0].shape[1]
    return pl.pallas_call(
        order_kernel,
        in_specs=[pl.BlockSpec(memory_space=pltpu.SMEM)] + [vmem] * len(parts),
        out_specs=vmem,
        out_shape=jax.ShapeDtypeStruct((total, cols), BF16),
        compiler_params=pltpu.CompilerParams(vmem_limit_bytes=8 << 20),
        name="order",
    )(place, *parts)


def local(sizes, orbitals, potential, rotation):
    doms, owners = sizes
    zs = doms
    ys = owners // zs
    states = orbitals.shape[0]
    me, spot = lax.axis_index("dom"), lax.axis_index("st")
    up = [(i, i + 1) for i in range(doms - 1)]
    down = [(i + 1, i) for i in range(doms - 1)]
    low_send, high_send = edges(
        pltpu.with_memory_space_constraint(orbitals, pltpu.HBM),
        pltpu.with_memory_space_constraint(potential, pltpu.HBM),
    )
    low = lax.ppermute(high_send, "dom", up)
    high = lax.ppermute(low_send, "dom", down)
    shift = [
        (d * owners + y * zs + z, d * owners + y * zs + (z + d) % zs)
        for d in range(doms)
        for y in range(ys)
        for z in range(zs)
    ]
    rotation, low_send = lax.optimization_barrier((rotation, low_send))
    rows = lax.ppermute(rotation, ("dom", "st"), shift)
    field, pot = prepare(orbitals, potential)
    rows, field = lax.optimization_barrier((rows, field))
    filtered = chebyshev(field, pot, low, high, owners, states)
    rows, _ = lax.optimization_barrier((rows, filtered))
    regrouped = lax.all_to_all(filtered, "st", split_axis=0, concat_axis=0, tiled=True)
    parts = [rows]
    swap = [(i, i ^ 1) for i in range(doms)]
    for perm, axis in (
        ([(i, (i + zs) % owners) for i in range(owners)], "st"),
        ([(i, (i + 2 * zs) % owners) for i in range(owners)], "st"),
        (swap, "dom"),
        ([(i, (i + 2) % doms) for i in range(doms)], "dom"),
        ([(i, (i + 4) % doms) for i in range(doms)], "dom"),
    ):
        parts.append(lax.ppermute(parts[0] if len(parts) == 1 else jnp.concatenate(parts), axis, perm))
    place = jnp.stack([me, spot // zs, spot % zs, jnp.int32(doms), jnp.int32(ys)])
    total = owners * states
    matrix = ordered(place, parts, total)
    return rotate(matrix, regrouped.reshape(total, regrouped.shape[2]))


def solution(mesh):
    sizes = (mesh.shape["dom"], mesh.shape["st"])
    return jax.shard_map(
        functools.partial(local, sizes),
        mesh=mesh,
        in_specs=(P("st", "dom", None), P("dom", None), P("st", None)),
        out_specs=P(None, ("dom", "st")),
        check_vma=False,
    )
```

```python
import functools

import jax
import jax.numpy as jnp
from jax import lax
from jax.experimental import pallas as pl
from jax.experimental.pallas import tpu as pltpu
from jax.sharding import PartitionSpec as P

DEGREE = 4
NZ = 32
LANES = 128

cheb_shift = 3.75
cheb_scale = 3.25

F32 = jnp.float32
BF16 = jnp.bfloat16

INNER_Y = LANES // NZ
RUN = NZ + 8
PLANE = INNER_Y * RUN


def one_hot(rows, cols, want):
    r = lax.broadcasted_iota(jnp.int32, (rows, cols), 0)
    c = lax.broadcasted_iota(jnp.int32, (rows, cols), 1)
    return jnp.where(c == want(r), 1.0, 0.0).astype(BF16)


def turned(block):
    eye = one_hot(LANES, LANES, lambda r: r)
    return lax.dot_general(eye, block, (((1,), (1,)), ((), ())), preferred_element_type=F32)


def stacked(rows, states, first, count):
    width = rows.shape[1]
    return jnp.concatenate(
        [
            rows[(first + p) * states : (first + p + 1) * states, j * LANES : (j + 1) * LANES]
            for p in range(count)
            for j in range(width // LANES)
        ],
        axis=0,
    )


def scaled(pot):
    return (pot - (cheb_shift - 3.0)) * 2.0


def edges_kernel(first_ref, last_ref, pot_first_ref, pot_last_ref, low_ref, high_ref):
    states, slab, width = first_ref.shape
    rows = DEGREE * states
    pick = one_hot(rows, states * slab, lambda r: (r % states) * slab + r // states)
    first = first_ref[...].reshape(states * slab, width)
    low_ref[:rows] = jnp.dot(pick, first, preferred_element_type=F32).astype(BF16)
    low_ref[rows:] = pot_first_ref[...]
    pick = one_hot(
        rows, states * slab, lambda r: (r % states) * slab + r // states + (slab - DEGREE)
    )
    last = last_ref[...].reshape(states * slab, width)
    high_ref[:rows] = jnp.dot(pick, last, preferred_element_type=F32).astype(BF16)
    high_ref[rows:] = pot_last_ref[...]


def edges(orbitals, potential):
    states, planes, width = orbitals.shape
    slab = 8
    last = planes // slab - 1
    out = jax.ShapeDtypeStruct((DEGREE * states + slab, width), BF16)
    return pl.pallas_call(
        edges_kernel,
        grid=(1,),
        in_specs=[
            pl.BlockSpec((states, slab, width), lambda i: (0, 0, 0)),
            pl.BlockSpec((states, slab, width), lambda i: (0, last, 0)),
            pl.BlockSpec((slab, width), lambda i: (0, 0)),
            pl.BlockSpec((slab, width), lambda i: (last, 0)),
        ],
        out_specs=[pl.BlockSpec(out.shape, lambda i: (0, 0))] * 2,
        out_shape=[out, out],
        compiler_params=pltpu.CompilerParams(vmem_limit_bytes=8 << 20),
        name="edges",
    )(orbitals, orbitals, potential, potential)


def spread(pot_rows, states):
    count = pot_rows.shape[0]
    repeat = one_hot(count * states, count, lambda r: r // states)
    return jnp.dot(repeat, pot_rows, preferred_element_type=F32).astype(BF16)


def prepare_kernel(x_ref, pot_ref, field_ref, pot_out_ref, select):
    states, group, width = x_ref.shape
    tiles = width // LANES

    @pl.when(pl.program_id(0) == 0)
    def _():
        r = lax.broadcasted_iota(jnp.int32, select.shape, 0)
        col = lax.broadcasted_iota(jnp.int32, select.shape, 1)
        want = (col % LANES) // states * group + col // LANES
        select[...] = jnp.where(r == want, 1.0, 0.0).astype(BF16)

    pick = one_hot(
        states * group, states * group, lambda r: (r % states) * group + r // states
    )
    rows = x_ref[...].reshape(states * group, width)
    pot = jnp.concatenate(
        [pot_ref[:, j * LANES : (j + 1) * LANES] for j in range(tiles)], axis=0
    )
    pot = turned(pot).astype(BF16)
    rows = jnp.dot(pick, rows, preferred_element_type=F32).astype(BF16)
    for p in range(0, group, 2):
        at = slice(p * LANES, (p + 2) * LANES)
        spreads = scaled(jnp.dot(pot, select[:, at], preferred_element_type=F32))
        both = turned(stacked(rows, states, p, 2)).astype(BF16)
        for source, target in ((both, field_ref), (spreads, pot_out_ref)):
            target[p] = source[:, :LANES]
            target[p + 1] = source[:, LANES:]


def prepare(orbitals, potential):
    states, planes, width = orbitals.shape
    group = 16
    out = jax.ShapeDtypeStruct((planes, LANES, LANES), BF16)
    return pl.pallas_call(
        prepare_kernel,
        grid=(planes // group,),
        in_specs=[
            pl.BlockSpec((states, group, width), lambda i: (0, i, 0)),
            pl.BlockSpec((group, width), lambda i: (i, 0)),
        ],
        out_specs=[pl.BlockSpec((group, LANES, LANES), lambda i: (i, 0, 0))] * 2,
        out_shape=[out, jax.ShapeDtypeStruct(out.shape, F32)],
        scratch_shapes=[pltpu.VMEM((group * width // LANES, group * LANES), BF16)],
        cost_estimate=pl.CostEstimate(
            flops=4 * 2 * states * planes * width * 256, transcendentals=0, bytes_accessed=8 << 20
        ),
        compiler_params=pltpu.CompilerParams(vmem_limit_bytes=16 << 20),
        name="prepare",
    )(orbitals, potential)


def filter_kernel(
    field_ref, pot_ref, low_ref, high_ref, out_hbm,
    even, odd, coef, done_ref, out_ref, out_sems,
):
    planes = field_ref.shape[0]
    owners, states, points = out_ref.shape
    width = LANES * (LANES // states)
    halo = DEGREE
    b = 1.0 / cheb_scale

    me, doms = lax.axis_index("dom"), lax.axis_size("dom")
    flags = (jnp.where(me > 0, 1.0, 0.0), jnp.where(me < doms - 1, 1.0, 0.0))
    def put(buffer, plane, values):
        for r in range(INNER_Y):
            at = pl.multiple_of(plane * PLANE + r * RUN + 8, 8)
            buffer[pl.ds(at, NZ), :] = values[r * NZ : (r + 1) * NZ]

    zero = jnp.zeros((8, LANES), F32)

    def clear(i, carry):
        for p in range(4):
            for r in range(INNER_Y):
                at = pl.multiple_of((i * 4 + p) * PLANE + r * RUN, 8)
                even[pl.ds(at, 8), :] = zero
                odd[pl.ds(at, 8), :] = zero
        return carry

    lax.fori_loop(0, (planes + 2 * halo) // 4, clear, 0)
    even[(planes + 2 * halo) * PLANE :, :] = zero
    odd[(planes + 2 * halo) * PLANE :, :] = zero

    rows = DEGREE * states
    for side, ref, base, at in ((0, low_ref, 0, 4), (1, high_ref, halo + planes, 0)):
        field = ref[:rows]
        pot = spread(ref[rows:], states)
        for p in range(0, halo, 2):
            both = turned(stacked(field, states, p, 2))
            put(even, base + p, both[:, :LANES])
            put(even, base + p + 1, both[:, LANES:])
            both = scaled(turned(stacked(pot, states, at + p, 2)))
            coef[side * halo + p] = both[:, :LANES]
            coef[side * halo + p + 1] = both[:, LANES:]

    for p in range(planes):
        put(even, halo + p, field_ref[p].astype(F32))

    lane = lax.broadcasted_iota(jnp.int32, (8, LANES), 1)
    first_y = lane < states
    last_y = lane >= LANES - states

    def sweep(k, first, count, together, factors, place, emit):
        src, dst = (even, odd) if k % 2 == 1 else (odd, even)
        base = pl.multiple_of(first * PLANE, 8)
        for start in range(0, NZ // 8, together):
            cols = range(start, start + together)

            def rows_at(n, r, q, offset=0):
                return src[pl.ds(base + (n * PLANE + r * RUN + 8 + q * 8 + offset), 8), :]

            def column(n):
                return {(r, q): rows_at(n, r, q) for q in cols for r in range(INNER_Y)}

            before, here = column(-1), column(0)
            for n in range(count):
                after = column(n + 1)
                for r in range(INNER_Y):
                    values = []
                    for q in cols:
                        v = here[r, q]
                        if r > 0:
                            below = here[r - 1, q]
                        else:
                            below = pltpu.roll(here[INNER_Y - 1, q], states, 1)
                            below = jnp.where(first_y, 0.0, below)
                        if r < INNER_Y - 1:
                            above = here[r + 1, q]
                        else:
                            above = pltpu.roll(here[0, q], LANES - states, 1)
                            above = jnp.where(last_y, 0.0, above)
                        along_z = rows_at(n, r, q, -1) + rows_at(n, r, q, 1)
                        along_x = before[r, q] + after[r, q]
                        at = r * NZ + q * 8
                        t = factors[place + n, at : at + 8, :] * v
                        t = t - ((below + above) + (along_z + along_x))
                        if k == 1:
                            values.append((0.5 * b) * t)
                        else:
                            at = base + (n * PLANE + r * RUN + 8 + q * 8)
                            values.append(b * t - dst[pl.ds(at, 8), :])
                    emit(n, r, start, values)
                before, here = here, after

    def store(k, first, flag=None):
        dst = odd if k % 2 == 1 else even
        base = pl.multiple_of(first * PLANE, 8)

        def emit(n, r, q, values):
            for i, v in enumerate(values):
                at = base + (n * PLANE + r * RUN + 8 + (q + i) * 8)
                dst[pl.ds(at, 8), :] = v if flag is None else v * flag

        return emit

    unroll = 8
    for k in range(1, DEGREE):
        def outer(i, carry, k=k):
            low_at, high_at = k + i, halo + planes + i
            sweep(k, low_at, 1, 1, coef, low_at, store(k, low_at, flags[0]))
            sweep(k, high_at, 1, 1, coef, halo + i, store(k, high_at, flags[1]))
            return carry

        lax.fori_loop(0, halo - k, outer, 0)

        def body(i, carry, k=k):
            first = halo + unroll * i
            sweep(k, first, unroll, 1, pot_ref, unroll * i, store(k, first))
            return carry

        lax.fori_loop(0, planes // unroll, body, 0)

    per = points // width
    batch = unroll // per

    def send(i):
        return pltpu.make_async_copy(
            out_ref.at[pl.ds(i * batch, batch)], out_hbm.at[pl.ds(i * batch, batch)], out_sems.at[i]
        )

    def finish(i):
        for n in range(batch):
            at = pl.multiple_of((i * batch + n) * per * LANES, per * LANES)
            out = turned(done_ref[pl.ds(at, per * LANES), :]).astype(BF16)
            for r in range(per):
                for j in range(width // LANES):
                    out_ref[
                        i * batch + n, :, r * width + j * LANES : r * width + (j + 1) * LANES
                    ] = out[j * states : (j + 1) * states, r * LANES : (r + 1) * LANES]

    def last(i):
        def emit(n, r, q, values):
            at = pl.multiple_of((unroll * i + n) * LANES + r * NZ + q * 8, 16)
            done_ref[pl.ds(at, 16), :] = jnp.concatenate(values, axis=0).astype(BF16)

        sweep(DEGREE, halo + unroll * i, unroll, 2, pot_ref, unroll * i, emit)

    def both(i, carry):
        finish(i - 1)
        last(i)
        send(i - 1).start()
        return carry

    count = planes // unroll
    last(0)
    lax.fori_loop(1, count, both, 0)
    finish(count - 1)
    send(count - 1).start()
    for i in range(count):
        send(i).wait()


def chebyshev(field, pot, low, high, owners, states):
    planes = field.shape[0]
    points = planes * LANES * LANES // states // owners
    total = planes + 2 * DEGREE
    hbm = pl.BlockSpec(memory_space=pltpu.HBM)
    return pl.pallas_call(
        filter_kernel,
        in_specs=[pl.BlockSpec(memory_space=pltpu.VMEM)] * 4,
        out_specs=hbm,
        out_shape=jax.ShapeDtypeStruct((owners, states, points), BF16),
        scratch_shapes=[
            pltpu.VMEM((total * PLANE + 8, LANES), F32),
            pltpu.VMEM((total * PLANE + 8, LANES), F32),
            pltpu.VMEM((2 * DEGREE, LANES, LANES), F32),
            pltpu.VMEM((planes * LANES, LANES), BF16),
            pltpu.VMEM((owners, states, points), BF16),
            pltpu.SemaphoreType.DMA((planes // 8,)),
        ],
        compiler_params=pltpu.CompilerParams(vmem_limit_bytes=59_300_000),
        name="chebyshev",
    )(*in_vmem(field, pot, low, high))


def rotate_kernel(r_ref, f_ref, out_hbm, out_ref, out_sems):
    tiles = out_ref.shape[0]
    tile = out_ref.shape[2]

    def give(i):
        return pltpu.make_async_copy(
            out_ref.at[i], out_hbm.at[:, pl.ds(i * tile, tile)], out_sems.at[i]
        )

    for i in range(tiles):
        part = f_ref[:, i * tile : (i + 1) * tile]
        out_ref[i] = jnp.dot(r_ref[...], part, preferred_element_type=F32).astype(BF16)
        give(i).start()
    for i in range(tiles):
        give(i).wait()


def in_vmem(*arrays):
    return [pltpu.with_memory_space_constraint(a, pltpu.VMEM) for a in arrays]


def rotate(rotation, filtered):
    total, points = filtered.shape
    tile = 256
    tiles = points // tile
    vmem = pl.BlockSpec(memory_space=pltpu.VMEM)
    return pl.pallas_call(
        rotate_kernel,
        in_specs=[vmem, vmem],
        out_specs=pl.BlockSpec(memory_space=pl.ANY),
        out_shape=jax.ShapeDtypeStruct((rotation.shape[0], points), BF16),
        scratch_shapes=[
            pltpu.VMEM((tiles, rotation.shape[0], tile), BF16),
            pltpu.SemaphoreType.DMA((tiles,)),
        ],
        compiler_params=pltpu.CompilerParams(vmem_limit_bytes=12 << 20),
        name="rotate",
    )(*in_vmem(rotation, filtered))


def order_kernel(place_ref, *refs):
    *parts, out_ref = refs
    dom, y, z = place_ref[0], place_ref[1], place_ref[2]
    doms, ys = place_ref[3], place_ref[4]
    total, cols = out_ref.shape
    own = parts[0].shape[0]
    r = lax.broadcasted_iota(jnp.int32, (8, total), 1) // own

    def bit(n):
        return (r >> n) & 1

    source = ((dom + 2 * doms - 4 * bit(4) - 2 * bit(3)) & (doms - 1)) ^ bit(2)
    zs = (z + doms - source) & (doms - 1)
    y_source = (y + 2 * ys - bit(0) - 2 * bit(1)) & (ys - 1)
    want = (y_source * doms + zs) * own
    want = want + lax.broadcasted_iota(jnp.int32, (8, total), 1) % own
    rows = lax.broadcasted_iota(jnp.int32, (total, total), 0)
    pick = jnp.where(rows == jnp.broadcast_to(want[:1], (total, total)), 1.0, 0.0).astype(BF16)
    gathered = jnp.concatenate([p[...] for p in parts], axis=0)
    out_ref[...] = jnp.dot(pick, gathered, preferred_element_type=F32).astype(BF16)


def ordered(place, parts, total):
    vmem = pl.BlockSpec(memory_space=pltpu.VMEM)
    cols = parts[0].shape[1]
    return pl.pallas_call(
        order_kernel,
        in_specs=[pl.BlockSpec(memory_space=pltpu.SMEM)] + [vmem] * len(parts),
        out_specs=vmem,
        out_shape=jax.ShapeDtypeStruct((total, cols), BF16),
        compiler_params=pltpu.CompilerParams(vmem_limit_bytes=8 << 20),
        name="order",
    )(place, *parts)


def local(sizes, orbitals, potential, rotation):
    doms, owners = sizes
    zs = doms
    ys = owners // zs
    states = orbitals.shape[0]
    me, spot = lax.axis_index("dom"), lax.axis_index("st")
    up = [(i, i + 1) for i in range(doms - 1)]
    down = [(i + 1, i) for i in range(doms - 1)]
    low_send, high_send = edges(
        pltpu.with_memory_space_constraint(orbitals, pltpu.HBM),
        pltpu.with_memory_space_constraint(potential, pltpu.HBM),
    )
    low = lax.ppermute(high_send, "dom", up)
    high = lax.ppermute(low_send, "dom", down)
    shift = [
        (d * owners + y * zs + z, d * owners + y * zs + (z + d) % zs)
        for d in range(doms)
        for y in range(ys)
        for z in range(zs)
    ]
    rotation, low_send = lax.optimization_barrier((rotation, low_send))
    rows = lax.ppermute(rotation, ("dom", "st"), shift)
    field, pot = prepare(orbitals, potential)
    rows, field = lax.optimization_barrier((rows, field))
    filtered = chebyshev(field, pot, low, high, owners, states)
    rows, _ = lax.optimization_barrier((rows, filtered))
    regrouped = lax.all_to_all(filtered, "st", split_axis=0, concat_axis=0, tiled=True)
    parts = [rows]
    swap = [(i, i ^ 1) for i in range(doms)]
    for perm, axis in (
        ([(i, (i + zs) % owners) for i in range(owners)], "st"),
        ([(i, (i + 2 * zs) % owners) for i in range(owners)], "st"),
        (swap, "dom"),
        ([(i, (i + 2) % doms) for i in range(doms)], "dom"),
        ([(i, (i + 4) % doms) for i in range(doms)], "dom"),
    ):
        parts.append(lax.ppermute(parts[0] if len(parts) == 1 else jnp.concatenate(parts), axis, perm))
    place = jnp.stack([me, spot // zs, spot % zs, jnp.int32(doms), jnp.int32(ys)])
    total = owners * states
    matrix = ordered(place, parts, total)
    return rotate(matrix, regrouped.reshape(total, regrouped.shape[2]))


def solution(mesh):
    sizes = (mesh.shape["dom"], mesh.shape["st"])
    return jax.shard_map(
        functools.partial(local, sizes),
        mesh=mesh,
        in_specs=(P("st", "dom", None), P("dom", None), P("st", None)),
        out_specs=P(None, ("dom", "st")),
        check_vma=False,
    )
```

```python
import functools

import jax
import jax.numpy as jnp
from jax import lax
from jax.experimental import pallas as pl
from jax.experimental.pallas import tpu as pltpu
from jax.sharding import PartitionSpec as P

DEGREE = 4
NZ = 32
LANES = 128

cheb_shift = 3.75
cheb_scale = 3.25

F32 = jnp.float32
BF16 = jnp.bfloat16

INNER_Y = LANES // NZ
RUN = NZ + 8
PLANE = INNER_Y * RUN


def one_hot(rows, cols, want):
    r = lax.broadcasted_iota(jnp.int32, (rows, cols), 0)
    c = lax.broadcasted_iota(jnp.int32, (rows, cols), 1)
    return jnp.where(c == want(r), 1.0, 0.0).astype(BF16)


def turned(block):
    eye = one_hot(LANES, LANES, lambda r: r)
    return lax.dot_general(eye, block, (((1,), (1,)), ((), ())), preferred_element_type=F32)


def stacked(rows, states, first, count):
    width = rows.shape[1]
    return jnp.concatenate(
        [
            rows[(first + p) * states : (first + p + 1) * states, j * LANES : (j + 1) * LANES]
            for p in range(count)
            for j in range(width // LANES)
        ],
        axis=0,
    )


def scaled(pot):
    return (pot - (cheb_shift - 3.0)) * 2.0


def edges_kernel(first_ref, last_ref, pot_first_ref, pot_last_ref, low_ref, high_ref):
    states, slab, width = first_ref.shape
    rows = DEGREE * states
    pick = one_hot(rows, states * slab, lambda r: (r % states) * slab + r // states)
    first = first_ref[...].reshape(states * slab, width)
    low_ref[:rows] = jnp.dot(pick, first, preferred_element_type=F32).astype(BF16)
    low_ref[rows:] = pot_first_ref[...]
    pick = one_hot(
        rows, states * slab, lambda r: (r % states) * slab + r // states + (slab - DEGREE)
    )
    last = last_ref[...].reshape(states * slab, width)
    high_ref[:rows] = jnp.dot(pick, last, preferred_element_type=F32).astype(BF16)
    high_ref[rows:] = pot_last_ref[...]


def edges(orbitals, potential):
    states, planes, width = orbitals.shape
    slab = 8
    last = planes // slab - 1
    out = jax.ShapeDtypeStruct((DEGREE * states + slab, width), BF16)
    return pl.pallas_call(
        edges_kernel,
        grid=(1,),
        in_specs=[
            pl.BlockSpec((states, slab, width), lambda i: (0, 0, 0)),
            pl.BlockSpec((states, slab, width), lambda i: (0, last, 0)),
            pl.BlockSpec((slab, width), lambda i: (0, 0)),
            pl.BlockSpec((slab, width), lambda i: (last, 0)),
        ],
        out_specs=[pl.BlockSpec(out.shape, lambda i: (0, 0))] * 2,
        out_shape=[out, out],
        compiler_params=pltpu.CompilerParams(vmem_limit_bytes=8 << 20),
        name="edges",
    )(orbitals, orbitals, potential, potential)


def spread(pot_rows, states):
    count = pot_rows.shape[0]
    repeat = one_hot(count * states, count, lambda r: r // states)
    return jnp.dot(repeat, pot_rows, preferred_element_type=F32).astype(BF16)


def prepare_kernel(x_ref, pot_ref, field_ref, pot_out_ref, select):
    states, group, width = x_ref.shape
    tiles = width // LANES

    @pl.when(pl.program_id(0) == 0)
    def _():
        r = lax.broadcasted_iota(jnp.int32, select.shape, 0)
        col = lax.broadcasted_iota(jnp.int32, select.shape, 1)
        want = (col % LANES) // states * group + col // LANES
        select[...] = jnp.where(r == want, 1.0, 0.0).astype(BF16)

    pick = one_hot(
        states * group, states * group, lambda r: (r % states) * group + r // states
    )
    rows = x_ref[...].reshape(states * group, width)
    pot = jnp.concatenate(
        [pot_ref[:, j * LANES : (j + 1) * LANES] for j in range(tiles)], axis=0
    )
    pot = turned(pot).astype(BF16)
    rows = jnp.dot(pick, rows, preferred_element_type=F32).astype(BF16)
    for p in range(0, group, 2):
        at = slice(p * LANES, (p + 2) * LANES)
        spreads = scaled(jnp.dot(pot, select[:, at], preferred_element_type=F32))
        both = turned(stacked(rows, states, p, 2)).astype(BF16)
        for source, target in ((both, field_ref), (spreads, pot_out_ref)):
            target[p] = source[:, :LANES]
            target[p + 1] = source[:, LANES:]


def prepare(orbitals, potential):
    states, planes, width = orbitals.shape
    group = 16
    out = jax.ShapeDtypeStruct((planes, LANES, LANES), BF16)
    return pl.pallas_call(
        prepare_kernel,
        grid=(planes // group,),
        in_specs=[
            pl.BlockSpec((states, group, width), lambda i: (0, i, 0)),
            pl.BlockSpec((group, width), lambda i: (i, 0)),
        ],
        out_specs=[pl.BlockSpec((group, LANES, LANES), lambda i: (i, 0, 0))] * 2,
        out_shape=[out, jax.ShapeDtypeStruct(out.shape, F32)],
        scratch_shapes=[pltpu.VMEM((group * width // LANES, group * LANES), BF16)],
        cost_estimate=pl.CostEstimate(
            flops=4 * 2 * states * planes * width * 256, transcendentals=0, bytes_accessed=8 << 20
        ),
        compiler_params=pltpu.CompilerParams(vmem_limit_bytes=16 << 20),
        name="prepare",
    )(orbitals, potential)


def filter_kernel(
    field_ref, pot_ref, low_ref, high_ref, out_hbm,
    even, odd, coef, done_ref, out_ref, out_sems,
):
    planes = field_ref.shape[0]
    owners, states, points = out_ref.shape
    width = LANES * (LANES // states)
    halo = DEGREE
    b = 1.0 / cheb_scale

    me, doms = lax.axis_index("dom"), lax.axis_size("dom")
    flags = (jnp.where(me > 0, 1.0, 0.0), jnp.where(me < doms - 1, 1.0, 0.0))
    def put(buffer, plane, values):
        for r in range(INNER_Y):
            at = pl.multiple_of(plane * PLANE + r * RUN + 8, 8)
            buffer[pl.ds(at, NZ), :] = values[r * NZ : (r + 1) * NZ]

    zero = jnp.zeros((8, LANES), F32)

    def clear(i, carry):
        for p in range(4):
            for r in range(INNER_Y):
                at = pl.multiple_of((i * 4 + p) * PLANE + r * RUN, 8)
                even[pl.ds(at, 8), :] = zero
                odd[pl.ds(at, 8), :] = zero
        return carry

    lax.fori_loop(0, (planes + 2 * halo) // 4, clear, 0)
    even[(planes + 2 * halo) * PLANE :, :] = zero
    odd[(planes + 2 * halo) * PLANE :, :] = zero

    rows = DEGREE * states
    for side, ref, base, at in ((0, low_ref, 0, 4), (1, high_ref, halo + planes, 0)):
        field = ref[:rows]
        pot = spread(ref[rows:], states)
        for p in range(0, halo, 2):
            both = turned(stacked(field, states, p, 2))
            put(even, base + p, both[:, :LANES])
            put(even, base + p + 1, both[:, LANES:])
            both = scaled(turned(stacked(pot, states, at + p, 2)))
            coef[side * halo + p] = both[:, :LANES]
            coef[side * halo + p + 1] = both[:, LANES:]

    for p in range(planes):
        put(even, halo + p, field_ref[p].astype(F32))

    lane = lax.broadcasted_iota(jnp.int32, (8, LANES), 1)
    first_y = lane < states
    last_y = lane >= LANES - states

    def sweep(k, first, count, together, factors, place, emit):
        src, dst = (even, odd) if k % 2 == 1 else (odd, even)
        base = pl.multiple_of(first * PLANE, 8)
        for start in range(0, NZ // 8, together):
            cols = range(start, start + together)

            def rows_at(n, r, q, offset=0):
                return src[pl.ds(base + (n * PLANE + r * RUN + 8 + q * 8 + offset), 8), :]

            def column(n):
                return {(r, q): rows_at(n, r, q) for q in cols for r in range(INNER_Y)}

            before, here = column(-1), column(0)
            for n in range(count):
                after = column(n + 1)
                for r in range(INNER_Y):
                    values = []
                    for q in cols:
                        v = here[r, q]
                        if r > 0:
                            below = here[r - 1, q]
                        else:
                            below = pltpu.roll(here[INNER_Y - 1, q], states, 1)
                            below = jnp.where(first_y, 0.0, below)
                        if r < INNER_Y - 1:
                            above = here[r + 1, q]
                        else:
                            above = pltpu.roll(here[0, q], LANES - states, 1)
                            above = jnp.where(last_y, 0.0, above)
                        along_z = rows_at(n, r, q, -1) + rows_at(n, r, q, 1)
                        along_x = before[r, q] + after[r, q]
                        at = r * NZ + q * 8
                        t = factors[place + n, at : at + 8, :] * v
                        t = t - ((below + above) + (along_z + along_x))
                        if k == 1:
                            values.append((0.5 * b) * t)
                        else:
                            at = base + (n * PLANE + r * RUN + 8 + q * 8)
                            values.append(b * t - dst[pl.ds(at, 8), :])
                    emit(n, r, start, values)
                before, here = here, after

    def store(k, first, flag=None):
        dst = odd if k % 2 == 1 else even
        base = pl.multiple_of(first * PLANE, 8)

        def emit(n, r, q, values):
            for i, v in enumerate(values):
                at = base + (n * PLANE + r * RUN + 8 + (q + i) * 8)
                dst[pl.ds(at, 8), :] = v if flag is None else v * flag

        return emit

    unroll = 8
    for k in range(1, DEGREE):
        def outer(i, carry, k=k):
            low_at, high_at = k + i, halo + planes + i
            sweep(k, low_at, 1, 1, coef, low_at, store(k, low_at, flags[0]))
            sweep(k, high_at, 1, 1, coef, halo + i, store(k, high_at, flags[1]))
            return carry

        lax.fori_loop(0, halo - k, outer, 0)

        def body(i, carry, k=k):
            first = halo + unroll * i
            sweep(k, first, unroll, 1, pot_ref, unroll * i, store(k, first))
            return carry

        lax.fori_loop(0, planes // unroll, body, 0)

    per = points // width
    batch = unroll // per

    def send(i):
        return pltpu.make_async_copy(
            out_ref.at[pl.ds(i * batch, batch)], out_hbm.at[pl.ds(i * batch, batch)], out_sems.at[i]
        )

    def finish(i):
        for n in range(batch):
            at = pl.multiple_of((i * batch + n) * per * LANES, per * LANES)
            out = turned(done_ref[pl.ds(at, per * LANES), :]).astype(BF16)
            for r in range(per):
                for j in range(width // LANES):
                    out_ref[
                        i * batch + n, :, r * width + j * LANES : r * width + (j + 1) * LANES
                    ] = out[j * states : (j + 1) * states, r * LANES : (r + 1) * LANES]

    def last(i):
        def emit(n, r, q, values):
            at = pl.multiple_of((unroll * i + n) * LANES + r * NZ + q * 8, 16)
            done_ref[pl.ds(at, 16), :] = jnp.concatenate(values, axis=0).astype(BF16)

        sweep(DEGREE, halo + unroll * i, unroll, 2, pot_ref, unroll * i, emit)

    def both(i, carry):
        finish(i - 1)
        last(i)
        send(i - 1).start()
        return carry

    count = planes // unroll
    last(0)
    lax.fori_loop(1, count, both, 0)
    finish(count - 1)
    send(count - 1).start()
    for i in range(count):
        send(i).wait()


def chebyshev(field, pot, low, high, owners, states):
    planes = field.shape[0]
    points = planes * LANES * LANES // states // owners
    total = planes + 2 * DEGREE
    hbm = pl.BlockSpec(memory_space=pltpu.HBM)
    return pl.pallas_call(
        filter_kernel,
        in_specs=[pl.BlockSpec(memory_space=pltpu.VMEM)] * 4,
        out_specs=hbm,
        out_shape=jax.ShapeDtypeStruct((owners, states, points), BF16),
        scratch_shapes=[
            pltpu.VMEM((total * PLANE + 8, LANES), F32),
            pltpu.VMEM((total * PLANE + 8, LANES), F32),
            pltpu.VMEM((2 * DEGREE, LANES, LANES), F32),
            pltpu.VMEM((planes * LANES, LANES), BF16),
            pltpu.VMEM((owners, states, points), BF16),
            pltpu.SemaphoreType.DMA((planes // 8,)),
        ],
        compiler_params=pltpu.CompilerParams(vmem_limit_bytes=59_300_000),
        name="chebyshev",
    )(*in_vmem(field, pot, low, high))


def rotate_kernel(r_ref, f_ref, out_hbm, out_ref, out_sems):
    tiles = out_ref.shape[0]
    tile = out_ref.shape[2]

    def give(i):
        return pltpu.make_async_copy(
            out_ref.at[i], out_hbm.at[:, pl.ds(i * tile, tile)], out_sems.at[i]
        )

    for i in range(tiles):
        part = f_ref[:, i * tile : (i + 1) * tile]
        out_ref[i] = jnp.dot(r_ref[...], part, preferred_element_type=F32).astype(BF16)
        give(i).start()
    for i in range(tiles):
        give(i).wait()


def in_vmem(*arrays):
    return [pltpu.with_memory_space_constraint(a, pltpu.VMEM) for a in arrays]


def rotate(rotation, filtered):
    total, points = filtered.shape
    tile = 256
    tiles = points // tile
    vmem = pl.BlockSpec(memory_space=pltpu.VMEM)
    return pl.pallas_call(
        rotate_kernel,
        in_specs=[vmem, vmem],
        out_specs=pl.BlockSpec(memory_space=pl.ANY),
        out_shape=jax.ShapeDtypeStruct((rotation.shape[0], points), BF16),
        scratch_shapes=[
            pltpu.VMEM((tiles, rotation.shape[0], tile), BF16),
            pltpu.SemaphoreType.DMA((tiles,)),
        ],
        compiler_params=pltpu.CompilerParams(vmem_limit_bytes=12 << 20),
        name="rotate",
    )(*in_vmem(rotation, filtered))


def order_kernel(place_ref, *refs):
    *parts, out_ref = refs
    dom, y, z = place_ref[0], place_ref[1], place_ref[2]
    doms, ys = place_ref[3], place_ref[4]
    total, cols = out_ref.shape
    own = parts[0].shape[0]
    r = lax.broadcasted_iota(jnp.int32, (8, total), 1) // own

    def bit(n):
        return (r >> n) & 1

    source = ((dom + 2 * doms - 4 * bit(4) - 2 * bit(3)) & (doms - 1)) ^ bit(2)
    zs = (z + doms - source) & (doms - 1)
    y_source = (y + 2 * ys - bit(0) - 2 * bit(1)) & (ys - 1)
    want = (y_source * doms + zs) * own
    want = want + lax.broadcasted_iota(jnp.int32, (8, total), 1) % own
    rows = lax.broadcasted_iota(jnp.int32, (total, total), 0)
    pick = jnp.where(rows == jnp.broadcast_to(want[:1], (total, total)), 1.0, 0.0).astype(BF16)
    gathered = jnp.concatenate([p[...] for p in parts], axis=0)
    out_ref[...] = jnp.dot(pick, gathered, preferred_element_type=F32).astype(BF16)


def ordered(place, parts, total):
    vmem = pl.BlockSpec(memory_space=pltpu.VMEM)
    cols = parts[0].shape[1]
    return pl.pallas_call(
        order_kernel,
        in_specs=[pl.BlockSpec(memory_space=pltpu.SMEM)] + [vmem] * len(parts),
        out_specs=vmem,
        out_shape=jax.ShapeDtypeStruct((total, cols), BF16),
        compiler_params=pltpu.CompilerParams(vmem_limit_bytes=8 << 20),
        name="order",
    )(place, *parts)


def local(sizes, orbitals, potential, rotation):
    doms, owners = sizes
    zs = doms
    ys = owners // zs
    states = orbitals.shape[0]
    me, spot = lax.axis_index("dom"), lax.axis_index("st")
    up = [(i, i + 1) for i in range(doms - 1)]
    down = [(i + 1, i) for i in range(doms - 1)]
    low_send, high_send = edges(
        pltpu.with_memory_space_constraint(orbitals, pltpu.HBM),
        pltpu.with_memory_space_constraint(potential, pltpu.HBM),
    )
    low = lax.ppermute(high_send, "dom", up)
    high = lax.ppermute(low_send, "dom", down)
    shift = [
        (d * owners + y * zs + z, d * owners + y * zs + (z + d) % zs)
        for d in range(doms)
        for y in range(ys)
        for z in range(zs)
    ]
    field, pot = prepare(orbitals, potential)
    rotation, field = lax.optimization_barrier((rotation, field))
    rows = lax.ppermute(rotation, ("dom", "st"), shift)
    filtered = chebyshev(field, pot, low, high, owners, states)
    rows, filtered = lax.optimization_barrier((rows, filtered))
    regrouped = lax.all_to_all(filtered, "st", split_axis=0, concat_axis=0, tiled=True)
    parts = [rows]
    swap = [(i, i ^ 1) for i in range(doms)]
    for perm, axis in (
        ([(i, (i + zs) % owners) for i in range(owners)], "st"),
        ([(i, (i + 2 * zs) % owners) for i in range(owners)], "st"),
        (swap, "dom"),
        ([(i, (i + 2) % doms) for i in range(doms)], "dom"),
        ([(i, (i + 4) % doms) for i in range(doms)], "dom"),
    ):
        parts.append(lax.ppermute(parts[0] if len(parts) == 1 else jnp.concatenate(parts), axis, perm))
    place = jnp.stack([me, spot // zs, spot % zs, jnp.int32(doms), jnp.int32(ys)])
    total = owners * states
    matrix = ordered(place, parts, total)
    return rotate(matrix, regrouped.reshape(total, regrouped.shape[2]))


def solution(mesh):
    sizes = (mesh.shape["dom"], mesh.shape["st"])
    return jax.shard_map(
        functools.partial(local, sizes),
        mesh=mesh,
        in_specs=(P("st", "dom", None), P("dom", None), P("st", None)),
        out_specs=P(None, ("dom", "st")),
        check_vma=False,
    )
```
